32 devices in a mesh: dp: 4 (over y, x), seq: 4 (over z), tensor: 2 (over core).
Axes of the slice: x: 2, y: 2, z: 4, core: 2. Of those that a mesh axis runs over, the one named last changes fastest.
Arguments:
- byte_ids: int32 [4, 4096], P('dp', 'seq'), may hold values from 0 to 255
- pad_lengths: int32 [4], P('dp'), may hold values from 0 to 2048
- table: bfloat16 [256, 2048], P(None, 'tensor'), may hold values from -6 to 6
- conv_weight: float32 [3, 2048], P(None, 'tensor'), may hold values from -4 to 4
- score_weight: float32 [2048], P('tensor'), may hold values from -0.25 to 0.25
- norm_gain: float32 [2048], P('tensor'), may hold values from 0.5 to 1.5
- query_weight: bfloat16 [2048, 1024], P('tensor'), may hold values from -0.125 to 0.125
- query_grad: bfloat16 [4, 2048, 1024], P('dp', 'seq'), may hold values from -6 to 6
Outputs:
- grad_table: bfloat16 [256, 2048], P(None, 'tensor')
- grad_conv: float32 [3, 2048], P(None, 'tensor')
- grad_score: float32 [2048], P('tensor')
- grad_gain: float32 [2048], P('tensor')
- grad_wq: bfloat16 [2048, 1024], P('tensor', 'seq')
The draws below stay inside these ranges and needn't reach their ends.
All inputs are finite; a program needn't handle non-finite values.
Results may differ from the reference program's by a relative error of at most 0.0095.
Values may be sent and summed in bfloat16 or wider, within the bound.
A program may use at most 128 MiB of HBM per device.

```python
import math
import jax
import jax.numpy as jnp
import numpy as np
from jax import lax

D = 2048
VOCAB = 256
BYTES_DEV = 1024
QW = 1024
DOCS = 4
BYTES = 4096
ROWS = 2048
N_SEQ = 4


def plant(entries, own_key, low, largest):
    shape = entries.shape
    place = [jax.random.randint(jax.random.fold_in(own_key, axis), (), 0, shape[axis]) for axis in range(len(shape))]
    entries = entries.at[tuple(place)].set(low)
    longest = shape.index(max(shape))
    place[longest] = (place[longest] + 1) % shape[longest]
    return entries.at[tuple(place)].set(largest)


def spiked(values, key, source, target, blocks, factor):
    owner, partner = [(jnp.arange(values.shape[position]) // (values.shape[position] // blocks)).reshape([-1 if axis == position else 1 for axis in range(values.ndim)]) for position in (source, target)]
    chosen = jax.random.permutation(key, blocks)[partner]
    strong = (owner == chosen) | (owner == (partner + blocks // 2) % blocks)
    return jnp.where(strong, factor * values, values)


def block_levels(rng, shape, split, smallest, largest):
    def one(position, shards_of):
        steps = jax.random.uniform(jax.random.fold_in(jax.random.fold_in(rng, 6), position), (shards_of,), jnp.float32, smallest / len(split), largest / len(split))
        return jnp.repeat(jnp.exp(steps), shape[position] // shards_of).reshape((-1,) + (1,) * (len(shape) - position - 1))

    level = one(*split[0])
    for cut in split[1:]:
        level = level * one(*cut)
    return level


def cumulative_ranks(number_of, slope):
    loads = [(1 << 20) // math.isqrt(rank ** slope) + 1 for rank in range(1, number_of + 1)]
    spread = 1 + sum(loads) // (1 << 30)
    return np.cumsum(np.array([max(1, weight // spread) for weight in loads]))


def skewed_ids(key, extent, count, skew):
    grid = cumulative_ranks(count, skew)
    ticket = jax.random.randint(jax.random.fold_in(key, 1), extent, 0, int(grid[count - 1]))
    rank = jnp.searchsorted(jnp.asarray(grid, jnp.int32), ticket, side="right")
    return jax.random.permutation(jax.random.fold_in(key, 2), count)[rank].astype(jnp.int32)


def noise(stream_key, extent, spread, reach, shards=(), held_as=jnp.bfloat16):
    gain = block_levels(stream_key, extent, shards, -0.22, 0.18) if shards else 1.0
    entries = jax.random.normal(stream_key, extent, jnp.float32) * spread * gain
    return jnp.minimum(jnp.maximum(entries, -reach), reach).astype(held_as)


def noise_with(key, shape, spread, reach, pieces, heavy, kind=jnp.bfloat16):
    array = spread * jax.random.normal(key, shape, jnp.float32)
    if pieces:
        array = array * block_levels(key, shape, pieces, -0.22, 0.18)
    return jnp.clip(spiked(array, jax.random.fold_in(key, 3), *heavy), -reach, reach).astype(kind)


def setup_inputs(seed: int = 0) -> dict:
    arg_keys = jax.random.split(jax.random.key(seed), 9)
    return {
        "byte_ids": plant(skewed_ids(arg_keys[0], (DOCS, BYTES), VOCAB, 2), jax.random.fold_in(arg_keys[0], 3), 0, VOCAB - 1).astype(jnp.int32),
        "pad_lengths": plant(jax.random.randint(arg_keys[1], (DOCS,), 0, BYTES // 2 + 1), jax.random.fold_in(arg_keys[1], 1), 0, (BYTES // 2 + 1) - 1).astype(jnp.int32),
        "table": noise(arg_keys[2], (VOCAB, D), 1.0, 6.0, ((1, 2),)),
        "conv_weight": noise(arg_keys[3], (3, D), 0.6, 4.0, ((1, 2),), jnp.float32),
        "score_weight": noise(arg_keys[4], (D,), (D // 4) ** -0.5, 0.25, ((0, 2),), jnp.float32),
        "norm_gain": jnp.clip(1.0 + 0.1 * jax.random.normal(arg_keys[5], (D,), jnp.float32), 0.5, 1.5),
        "query_weight": noise(arg_keys[6], (D, QW), D ** -0.5, 0.125, ((0, 2),)),
        "query_grad": noise_with(arg_keys[7], (DOCS, ROWS, QW), 1.0, 6.0, ((0, 4), (1, 4)), (1, 2, 4, 2.0)),
    }


EPS = 1e-06

def block_means(rows, width):
    count = rows.shape[0]
    chans = rows.shape[1]
    grouped = lax.optimization_barrier(jnp.mean(rows.reshape(count // width, width, chans), axis=1))
    return jnp.repeat(grouped, width, axis=0)

def piece_normed(embed, conv_weight, score_weight, norm_gain, start):
    count = embed.shape[0] - 6
    pos_c = start + jnp.arange(-2, count + 2, dtype=jnp.int32)
    valid_c = ((pos_c >= 0) & (pos_c < BYTES)).astype(jnp.float32)[:, None]
    conv = (conv_weight[0] * embed[0:count + 4] + conv_weight[1] * embed[1:count + 5] + conv_weight[2] * embed[2:count + 6]) * valid_c
    own = conv[2:count + 2]
    resid = (start + jnp.arange(count, dtype=jnp.int32)) % 3
    third = jnp.zeros_like(own)
    for shift in range(-2, 3):
        keep = ((resid >= -shift) & (resid <= 2 - shift)).astype(jnp.float32)[:, None]
        third = third + keep * conv[2 + shift:2 + shift + count] / 3.0
    cands = [own, block_means(own, 2), third, block_means(own, 4)]
    scores = jnp.stack([lax.optimization_barrier(jnp.sum(cand * score_weight, axis=1)) for cand in cands])
    expo = jnp.exp(scores)
    probs = expo / lax.optimization_barrier(jnp.sum(expo, axis=0, keepdims=True))
    mixed = probs[0][:, None] * cands[0]
    for block in range(1, 4):
        mixed = mixed + probs[block][:, None] * cands[block]
    pooled = lax.optimization_barrier(jnp.mean(mixed.reshape(count // 2, 2, mixed.shape[1]), axis=1))
    scale = lax.rsqrt(lax.optimization_barrier(jnp.mean(pooled * pooled, axis=1)) + EPS)[:, None]
    return pooled * scale * norm_gain

def reference(byte_ids, pad_lengths, table, conv_weight, score_weight, norm_gain, query_weight, query_grad):
    table_f = table.astype(jnp.float32)
    padded_ids = jnp.pad(byte_ids, ((0, 0), (3, 3)))
    half = BYTES_DEV // 2

    def one_piece(carry, item):
        table_acc, conv_acc, score_acc, gain_acc, query_acc = carry
        doc = (item // N_SEQ).astype(jnp.int32)
        start = (item % N_SEQ * BYTES_DEV).astype(jnp.int32)
        ids_ext = lax.dynamic_slice(padded_ids, (doc, start), (1, BYTES_DEV + 6))[0]
        limit = BYTES - pad_lengths[doc]
        pos_e = start + jnp.arange(-3, BYTES_DEV + 3, dtype=jnp.int32)
        valid_e = ((pos_e >= 0) & (pos_e < limit)).astype(jnp.float32)[:, None]
        embed = table_f[ids_ext] * valid_e
        row_pos = start // 2 + jnp.arange(half, dtype=jnp.int32)
        row_keep = (2 * row_pos < limit)[:, None]
        grads = lax.dynamic_slice(query_grad, (doc, start // 2, jnp.int32(0)), (1, half, QW))[0]
        grads = jnp.where(row_keep, grads, jnp.zeros_like(grads))

        def forward(emb, cw, sw, ng):
            return piece_normed(emb, cw, sw, ng, start)
        normed_f, pull = jax.vjp(forward, embed, conv_weight, score_weight, norm_gain)
        normed_grad = jnp.dot(grads, query_weight.T, preferred_element_type=jnp.float32)
        d_embed, d_conv, d_score, d_gain = pull(normed_grad)
        table_acc = table_acc.at[ids_ext].add(d_embed * valid_e)
        normed = normed_f.astype(jnp.bfloat16)
        query_acc = query_acc + jnp.dot(normed.T, grads, preferred_element_type=jnp.float32)
        return ((table_acc, conv_acc + d_conv, score_acc + d_score, gain_acc + d_gain, query_acc), None)
    init = (jnp.zeros((VOCAB, D), jnp.float32), jnp.zeros((3, D), jnp.float32), jnp.zeros((D,), jnp.float32), jnp.zeros((D,), jnp.float32), jnp.zeros((D, QW), jnp.float32))
    final, unused = lax.scan(one_piece, init, jnp.arange(DOCS * N_SEQ, dtype=jnp.int32))
    table_acc, conv_acc, score_acc, gain_acc, query_acc = final
    return (table_acc.astype(jnp.bfloat16), conv_acc, score_acc, gain_acc, query_acc.astype(jnp.bfloat16))
```

```python
import functools

import jax
import jax.numpy as jnp
from jax import lax
from jax.experimental import pallas as pl
from jax.experimental.pallas import tpu as pltpu
from jax.sharding import PartitionSpec as P

D = 2048
EPS = 1e-06
F32 = jnp.float32
BF16 = jnp.bfloat16
OFFS = range(-2, 4)
CHUNK = 256

NN = (((1,), (0,)), ((), ()))
NT = (((1,), (1,)), ((), ()))
TN = (((0,), (0,)), ((), ()))


def mm(lhs, rhs, dims):
    return lax.dot_general(lhs, rhs, dims, preferred_element_type=F32)


def block_weights(start, total, rows):
    i = lax.broadcasted_iota(jnp.int32, (1, rows), 1)
    even = (i % 2) == 0
    inside = {o: (start + 2 * i + o >= 0) & (start + 2 * i + o < total) for o in OFFS}
    table = []
    for b in range(4):
        for p in range(2):
            row = {}
            for o in OFFS:
                if b == 0:
                    if o == p:
                        row[o] = jnp.where(inside[o], 1.0, 0.0)
                elif b == 1:
                    if o in (0, 1):
                        row[o] = jnp.where(inside[o], 0.5, 0.0)
                elif b == 3:
                    if o in (0, 1):
                        row[o] = jnp.where(inside[o], 0.25, 0.0)
                    else:
                        row[o] = jnp.where(inside[o] & (even if o > 1 else ~even), 0.25, 0.0)
                else:
                    d = o - p
                    if -2 <= d <= 2:
                        r = (start + 2 * i + p) % 3
                        row[o] = jnp.where(inside[o] & (r >= -d) & (r <= 2 - d), 1.0 / 3.0, 0.0)
            table.append(row)
    return table


def spread(idm, rows_of, tap):
    rows = idm.shape[1]
    v = lax.broadcasted_iota(jnp.int32, (256, rows), 0)
    acc = None
    for o in OFFS:
        at = o + tap + 2
        term = jnp.where(idm[at : at + 1, :] == v, rows_of[o], 0.0)
        acc = term if acc is None else acc + term
    return acc


def forward_kernel(
    pos_ref, idm_ref, p_ref, table_ref, cw_ref, gain_ref, wq_ref, g_ref,
    pooled_ref, ng_ref, wt_ref, sums_ref, rows_ref, grads_ref,
    wh, wl, r1, r2, sq, rd,
):
    start, limit, total = pos_ref[0], pos_ref[1], pos_ref[2]
    rows = idm_ref.shape[1]
    chans = table_ref.shape[1]
    idm = idm_ref[...]
    v = lax.broadcasted_iota(jnp.int32, (256, rows), 0)
    p = p_ref[...]
    hi = p.astype(BF16)
    rest = p - hi.astype(F32)
    mid = rest.astype(BF16)
    low = (rest - mid.astype(F32)).astype(BF16)
    p3 = jnp.concatenate([hi.astype(F32), mid.astype(F32), low.astype(F32)], axis=0).astype(BF16)
    picks = []
    for j in range(8):
        hot = jnp.where(idm[j : j + 1, :] == v, 1.0, 0.0).astype(BF16)
        g = mm(p3, hot, NN)
        picks.append(g[0:8] + g[8:16] + g[16:24])
    s = {o: picks[o + 2][0:1] + picks[o + 3][1:2] + picks[o + 4][2:3] for o in OFFS}
    weights = block_weights(start, total, rows)
    expo = []
    for row in weights:
        score = None
        for o in row:
            score = row[o] * s[o] if score is None else score + row[o] * s[o]
        expo.append(jnp.exp(score))
    probs = []
    for n in range(8):
        whole = expo[n % 2] + expo[2 + n % 2] + expo[4 + n % 2] + expo[6 + n % 2]
        probs.append(expo[n] / whole)
    a = {}
    for o in OFFS:
        acc = None
        for n in range(8):
            if o in weights[n]:
                term = probs[n] * weights[n][o]
                acc = term if acc is None else acc + term
        a[o] = 0.5 * acc
    rows_ref[...] = jnp.concatenate(probs, axis=0)
    for k in range(3):
        w = spread(idm, a, k)
        wt_ref[k] = w.astype(BF16)
        wf = w.T
        top = wf.astype(BF16)
        wh[k] = top
        wl[k] = (wf - top.astype(F32)).astype(BF16)
    keep = (start + 2 * lax.broadcasted_iota(jnp.int32, g_ref.shape, 0)) < limit
    grads_ref[...] = jnp.where(keep, g_ref[...].astype(F32), 0.0).astype(BF16)
    r1[...] = jnp.zeros_like(r1)
    r2[...] = jnp.zeros_like(r2)
    sq[...] = jnp.zeros_like(sq)
    rd[...] = jnp.zeros_like(rd)

    def step(c, carry):
        at = pl.ds(pl.multiple_of(c * CHUNK, CHUNK), CHUNK)
        tab = table_ref[:, at]
        cw = cw_ref[:, at]
        ng = mm(grads_ref[...], wq_ref[at, :], NT)
        pooled = None
        for k in range(3):
            part = cw[k : k + 1] * (mm(wh[k], tab, NN) + mm(wl[k], tab, NN))
            pooled = part if pooled is None else pooled + part
        pooled_ref[:, at] = pooled
        ng_ref[:, at] = ng
        gained = ng * gain_ref[:, at]
        square = pooled * pooled
        inner = pooled * gained
        sq[...] += square[:, 0:128] + square[:, 128:256]
        rd[...] += inner[:, 0:128] + inner[:, 128:256]
        gb = gained.astype(BF16)
        pb = pooled.astype(BF16)
        for k in range(3):
            tk = (tab.astype(F32) * cw[k : k + 1]).astype(BF16)
            r1[k] += mm(tk, gb, NT)
            r2[k] += mm(tk, pb, NT)
        return carry

    lax.fori_loop(0, chans // CHUNK, step, 0)
    out = []
    for r in (r1, r2):
        for o in OFFS:
            acc = None
            for k in range(3):
                at = o + k + 2
                term = jnp.where(idm[at : at + 1, :] == v, r[k], 0.0)
                acc = term if acc is None else acc + term
            out.append(jnp.sum(acc, axis=0, keepdims=True))
    out.append(jnp.sum(sq[...].T, axis=0, keepdims=True))
    out.append(jnp.sum(rd[...].T, axis=0, keepdims=True))
    out.append(jnp.zeros((2, rows), F32))
    sums_ref[...] = jnp.concatenate(out, axis=0)


def backward_kernel(
    pos_ref, idm_ref, sums_ref, rows_ref, table_ref, cw_ref, sw_ref, gain_ref,
    pooled_ref, ng_ref, wt_ref, grads_ref,
    query_ref, tab_ref, small_ref,
):
    start, total = pos_ref[0], pos_ref[2]
    rows = idm_ref.shape[1]
    chans = table_ref.shape[1]
    idm = idm_ref[...]
    sums = sums_ref[...]
    probs = rows_ref[...]
    square, inner = sums[12:13], sums[13:14]
    scale = lax.rsqrt(square / D + EPS)
    pull = scale * scale * scale * (inner / D)
    q = {o: scale * sums[o + 2 : o + 3] - pull * sums[o + 8 : o + 9] for o in OFFS}
    weights = block_weights(start, total, rows)
    pgrad = []
    for row in weights:
        acc = None
        for o in row:
            acc = row[o] * q[o] if acc is None else acc + row[o] * q[o]
        pgrad.append(0.5 * acc)
    sgrad = []
    for n in range(8):
        mean = None
        for m in range(n % 2, 8, 2):
            term = probs[m : m + 1] * pgrad[m]
            mean = term if mean is None else mean + term
        sgrad.append(probs[n : n + 1] * (pgrad[n] - mean))
    ds = {}
    for o in OFFS:
        acc = None
        for n in range(8):
            if o in weights[n]:
                term = sgrad[n] * weights[n][o]
                acc = term if acc is None else acc + term
        ds[o] = acc
    hist = [jnp.sum(spread(idm, ds, k), axis=1, keepdims=True) for k in range(3)]
    cols = jnp.concatenate([scale, pull, jnp.zeros((6, rows), F32)], axis=0).T
    scale_c, pull_c = cols[:, 0:1], cols[:, 1:2]

    for c in range(chans // CHUNK):
        at = pl.ds(c * CHUNK, CHUNK)
        tab = table_ref[:, at].astype(F32)
        cw = cw_ref[:, at]
        sw = sw_ref[:, at]
        gain = gain_ref[:, at]
        ps = pooled_ref[:, at] * scale_c
        ng = ng_ref[:, at]
        gain_term = jnp.sum(ng * ps, axis=0, keepdims=True)
        normed = (ps * gain).astype(BF16)
        query_ref[at, :] = mm(normed, grads_ref[...], TN).astype(query_ref.dtype)
        pg = (ng * gain * scale_c - pull_c * pooled_ref[:, at]).astype(BF16)
        total_t = None
        outs = []
        score = None
        for k in range(3):
            full = mm(wt_ref[k], pg, NN) + hist[k] * sw
            term = cw[k : k + 1] * full
            total_t = term if total_t is None else total_t + term
            outs.append(jnp.sum(full * tab, axis=0, keepdims=True))
            term = cw[k : k + 1] * jnp.sum(hist[k] * tab, axis=0, keepdims=True)
            score = term if score is None else score + term
        tab_ref[:, at] = total_t.astype(tab_ref.dtype)
        small_ref[:, at] = jnp.concatenate(
            outs + [score, gain_term, jnp.zeros((3, CHUNK), F32)], axis=0
        )


def body(
    byte_ids, pad_lengths, table, conv_weight, score_weight, norm_gain, query_weight, query_grad
):
    ids = byte_ids[0]
    count = ids.shape[0]
    rows = count // 2
    vocab, chans = table.shape
    width = query_grad.shape[2]
    n_seq = lax.axis_size("seq")
    total = count * n_seq
    start = lax.axis_index("seq") * count
    limit = total - pad_lengths[0]
    ends = n_seq - 1
    up = [(i, i + 1) for i in range(ends)]
    down = [(i + 1, i) for i in range(ends)]
    ids_ext = jnp.concatenate(
        [lax.ppermute(ids[count - 3 :], "seq", up), ids, lax.ppermute(ids[:3], "seq", down)]
    )
    pos_e = start + jnp.arange(-3, count + 3, dtype=jnp.int32)
    ids_ext = jnp.where((pos_e >= 0) & (pos_e < limit), ids_ext, -1)
    halves = ids_ext.reshape(rows + 3, 2).T
    idm = jnp.stack([halves[j % 2, j // 2 : j // 2 + rows] for j in range(8)])
    pos = jnp.stack([start, limit, jnp.full_like(start, total)]).astype(jnp.int32)

    part = jnp.dot(
        conv_weight * score_weight, table.astype(F32).T, precision=lax.Precision.HIGHEST
    )
    p = jnp.pad(lax.psum(part, "tensor"), ((0, 5), (0, 0)))

    vm = pl.BlockSpec(memory_space=pltpu.VMEM)
    sm = pl.BlockSpec(memory_space=pltpu.SMEM)
    sw = score_weight[None, :]
    gain = norm_gain[None, :]
    pooled, ng, wt, sums, probs, grads = pl.pallas_call(
        forward_kernel,
        out_shape=(
            jax.ShapeDtypeStruct((rows, chans), F32),
            jax.ShapeDtypeStruct((rows, chans), F32),
            jax.ShapeDtypeStruct((3, vocab, rows), BF16),
            jax.ShapeDtypeStruct((16, rows), F32),
            jax.ShapeDtypeStruct((8, rows), F32),
            jax.ShapeDtypeStruct((rows, width), BF16),
        ),
        in_specs=[sm] + [vm] * 7,
        out_specs=(vm,) * 6,
        scratch_shapes=[
            pltpu.VMEM((3, rows, vocab), BF16),
            pltpu.VMEM((3, rows, vocab), BF16),
            pltpu.VMEM((3, vocab, rows), F32),
            pltpu.VMEM((3, vocab, rows), F32),
            pltpu.VMEM((rows, 128), F32),
            pltpu.VMEM((rows, 128), F32),
        ],
        name="forward",
    )(pos, idm, p, table, conv_weight, gain, query_weight, query_grad[0])
    sums = lax.psum(sums, "tensor")
    query, tab, small = pl.pallas_call(
        backward_kernel,
        out_shape=(
            jax.ShapeDtypeStruct((chans, width), BF16),
            jax.ShapeDtypeStruct((vocab, chans), BF16),
            jax.ShapeDtypeStruct((8, chans), F32),
        ),
        in_specs=[sm] + [vm] * 11,
        out_specs=(vm,) * 3,
        name="backward",
    )(pos, idm, sums, probs, table, conv_weight, sw, gain, pooled, ng, wt, grads)

    share = lax.psum_scatter(query, "seq", scatter_dimension=1, tiled=True)
    query_out = lax.psum(share, "dp")
    tab_out = lax.psum(tab, ("dp", "seq"))
    small_out = lax.psum(small, ("dp", "seq"))
    return (tab_out, small_out[0:3], small_out[3], small_out[4], query_out)


def solution(mesh):
    return jax.shard_map(
        body,
        mesh=mesh,
        in_specs=(
            P("dp", "seq"),
            P("dp"),
            P(None, "tensor"),
            P(None, "tensor"),
            P("tensor"),
            P("tensor"),
            P("tensor", None),
            P("dp", "seq", None),
        ),
        out_specs=(
            P(None, "tensor"),
            P(None, "tensor"),
            P("tensor"),
            P("tensor"),
            P("tensor", "seq"),
        ),
        check_vma=False,
    )
```

```python
import functools

import jax
import jax.numpy as jnp
from jax import lax
from jax.experimental import pallas as pl
from jax.experimental.pallas import tpu as pltpu
from jax.sharding import PartitionSpec as P

D = 2048
EPS = 1e-06
F32 = jnp.float32
BF16 = jnp.bfloat16
OFFS = range(-2, 4)
CHUNK = 256

NN = (((1,), (0,)), ((), ()))
NT = (((1,), (1,)), ((), ()))
TN = (((0,), (0,)), ((), ()))


def mm(lhs, rhs, dims):
    return lax.dot_general(lhs, rhs, dims, preferred_element_type=F32)


def block_weights(start, total, rows):
    i = lax.broadcasted_iota(jnp.int32, (1, rows), 1)
    even = (i % 2) == 0
    inside = {o: (start + 2 * i + o >= 0) & (start + 2 * i + o < total) for o in OFFS}
    table = []
    for b in range(4):
        for p in range(2):
            row = {}
            for o in OFFS:
                if b == 0:
                    if o == p:
                        row[o] = jnp.where(inside[o], 1.0, 0.0)
                elif b == 1:
                    if o in (0, 1):
                        row[o] = jnp.where(inside[o], 0.5, 0.0)
                elif b == 3:
                    if o in (0, 1):
                        row[o] = jnp.where(inside[o], 0.25, 0.0)
                    else:
                        row[o] = jnp.where(inside[o] & (even if o > 1 else ~even), 0.25, 0.0)
                else:
                    d = o - p
                    if -2 <= d <= 2:
                        r = (start + 2 * i + p) % 3
                        row[o] = jnp.where(inside[o] & (r >= -d) & (r <= 2 - d), 1.0 / 3.0, 0.0)
            table.append(row)
    return table


def spread(idm, rows_of, tap):
    rows = idm.shape[1]
    v = lax.broadcasted_iota(jnp.int32, (256, rows), 0)
    acc = None
    for o in OFFS:
        at = o + tap + 2
        term = jnp.where(idm[at : at + 1, :] == v, rows_of[o], 0.0)
        acc = term if acc is None else acc + term
    return acc


def forward_kernel(
    pos_ref, idm_ref, p_ref, table_ref, cw_ref, gain_ref, wq_ref, g_ref,
    pooled_ref, ng_ref, wt_ref, sums_ref, rows_ref, grads_ref,
    wh, wl, r1, r2, sq, rd,
):
    start, limit, total = pos_ref[0], pos_ref[1], pos_ref[2]
    rows = idm_ref.shape[1]
    chans = table_ref.shape[1]
    idm = idm_ref[...]
    v = lax.broadcasted_iota(jnp.int32, (256, rows), 0)
    p = p_ref[...]
    hi = p.astype(BF16)
    rest = p - hi.astype(F32)
    mid = rest.astype(BF16)
    low = (rest - mid.astype(F32)).astype(BF16)
    p3 = jnp.concatenate([hi.astype(F32), mid.astype(F32), low.astype(F32)], axis=0).astype(BF16)
    picks = []
    for j in range(8):
        hot = jnp.where(idm[j : j + 1, :] == v, 1.0, 0.0).astype(BF16)
        g = mm(p3, hot, NN)
        picks.append(g[0:8] + g[8:16] + g[16:24])
    s = {o: picks[o + 2][0:1] + picks[o + 3][1:2] + picks[o + 4][2:3] for o in OFFS}
    weights = block_weights(start, total, rows)
    expo = []
    for row in weights:
        score = None
        for o in row:
            score = row[o] * s[o] if score is None else score + row[o] * s[o]
        expo.append(jnp.exp(score))
    probs = []
    for n in range(8):
        whole = expo[n % 2] + expo[2 + n % 2] + expo[4 + n % 2] + expo[6 + n % 2]
        probs.append(expo[n] / whole)
    a = {}
    for o in OFFS:
        acc = None
        for n in range(8):
            if o in weights[n]:
                term = probs[n] * weights[n][o]
                acc = term if acc is None else acc + term
        a[o] = 0.5 * acc
    rows_ref[...] = jnp.concatenate(probs, axis=0)
    for k in range(3):
        w = spread(idm, a, k)
        wt_ref[k] = w.astype(BF16)
        wf = w.T
        top = wf.astype(BF16)
        wh[k] = top
        wl[k] = (wf - top.astype(F32)).astype(BF16)
    keep = (start + 2 * lax.broadcasted_iota(jnp.int32, g_ref.shape, 0)) < limit
    grads_ref[...] = jnp.where(keep, g_ref[...].astype(F32), 0.0).astype(BF16)
    r1[...] = jnp.zeros_like(r1)
    r2[...] = jnp.zeros_like(r2)
    sq[...] = jnp.zeros_like(sq)
    rd[...] = jnp.zeros_like(rd)

    def step(c, carry):
        at = pl.ds(pl.multiple_of(c * CHUNK, CHUNK), CHUNK)
        tab = table_ref[:, at]
        cw = cw_ref[:, at]
        ng = mm(grads_ref[...], wq_ref[at, :], NT)
        pooled = None
        for k in range(3):
            part = cw[k : k + 1] * (mm(wh[k], tab, NN) + mm(wl[k], tab, NN))
            pooled = part if pooled is None else pooled + part
        pooled_ref[:, at] = pooled
        ng_ref[:, at] = ng
        gained = ng * gain_ref[:, at]
        square = pooled * pooled
        inner = pooled * gained
        sq[...] += square[:, 0:128] + square[:, 128:256]
        rd[...] += inner[:, 0:128] + inner[:, 128:256]
        gb = gained.astype(BF16)
        pb = pooled.astype(BF16)
        for k in range(3):
            tk = (tab.astype(F32) * cw[k : k + 1]).astype(BF16)
            r1[k] += mm(tk, gb, NT)
            r2[k] += mm(tk, pb, NT)
        return carry

    lax.fori_loop(0, chans // CHUNK, step, 0)
    out = []
    for r in (r1, r2):
        for o in OFFS:
            acc = None
            for k in range(3):
                at = o + k + 2
                term = jnp.where(idm[at : at + 1, :] == v, r[k], 0.0)
                acc = term if acc is None else acc + term
            out.append(jnp.sum(acc, axis=0, keepdims=True))
    out.append(jnp.sum(sq[...].T, axis=0, keepdims=True))
    out.append(jnp.sum(rd[...].T, axis=0, keepdims=True))
    out.append(jnp.zeros((2, rows), F32))
    sums_ref[...] = jnp.concatenate(out, axis=0)


def backward_kernel(
    pos_ref, idm_ref, sums_ref, rows_ref, table_ref, cw_ref, sw_ref, gain_ref,
    pooled_ref, ng_ref, wt_ref, grads_ref,
    *out_refs,
):
    small_ref = out_refs[-1]
    packed = len(out_refs) == 2
    start, total = pos_ref[0], pos_ref[2]
    rows = idm_ref.shape[1]
    chans = table_ref.shape[1]
    idm = idm_ref[...]
    sums = sums_ref[...]
    probs = rows_ref[...]
    square, inner = sums[12:13], sums[13:14]
    scale = lax.rsqrt(square / D + EPS)
    pull = scale * scale * scale * (inner / D)
    q = {o: scale * sums[o + 2 : o + 3] - pull * sums[o + 8 : o + 9] for o in OFFS}
    weights = block_weights(start, total, rows)
    pgrad = []
    for row in weights:
        acc = None
        for o in row:
            acc = row[o] * q[o] if acc is None else acc + row[o] * q[o]
        pgrad.append(0.5 * acc)
    sgrad = []
    for n in range(8):
        mean = None
        for m in range(n % 2, 8, 2):
            term = probs[m : m + 1] * pgrad[m]
            mean = term if mean is None else mean + term
        sgrad.append(probs[n : n + 1] * (pgrad[n] - mean))
    ds = {}
    for o in OFFS:
        acc = None
        for n in range(8):
            if o in weights[n]:
                term = sgrad[n] * weights[n][o]
                acc = term if acc is None else acc + term
        ds[o] = acc
    hist = [jnp.sum(spread(idm, ds, k), axis=1, keepdims=True) for k in range(3)]
    cols = jnp.concatenate([scale, pull, jnp.zeros((6, rows), F32)], axis=0).T
    scale_c, pull_c = cols[:, 0:1], cols[:, 1:2]

    for c in range(chans // CHUNK):
        at = pl.ds(c * CHUNK, CHUNK)
        tab = table_ref[:, at].astype(F32)
        cw = cw_ref[:, at]
        sw = sw_ref[:, at]
        gain = gain_ref[:, at]
        ps = pooled_ref[:, at] * scale_c
        ng = ng_ref[:, at]
        gain_term = jnp.sum(ng * ps, axis=0, keepdims=True)
        normed = (ps * gain).astype(BF16)
        query = mm(normed, grads_ref[...], TN).astype(BF16)
        if packed:
            for zb in range(4):
                for n in range(2):
                    out_refs[0][zb, 2 * c + n, 0:128, :] = query[
                        128 * n : 128 * n + 128, 256 * zb : 256 * zb + 256
                    ]
        else:
            out_refs[0][at, :] = query
        pg = (ng * gain * scale_c - pull_c * pooled_ref[:, at]).astype(BF16)
        total_t = None
        outs = []
        score = None
        for k in range(3):
            full = mm(wt_ref[k], pg, NN) + hist[k] * sw
            term = cw[k : k + 1] * full
            total_t = term if total_t is None else total_t + term
            outs.append(jnp.sum(full * tab, axis=0, keepdims=True))
            term = cw[k : k + 1] * jnp.sum(hist[k] * tab, axis=0, keepdims=True)
            score = term if score is None else score + term
        total_t = total_t.astype(BF16)
        if packed:
            for n in range(8):
                out_refs[0][c, n, 128:160, :] = total_t[32 * n : 32 * n + 32, :]
        else:
            out_refs[1][:, at] = total_t
        small_ref[:, at] = jnp.concatenate(
            outs + [score, gain_term, jnp.zeros((3, CHUNK), F32)], axis=0
        )


def reduce_kernel(
    u, small, outq, outt, outs,
    r1, a1, r2, a2, r3, sb1, sb2,
    s1s, s1r, s2s, s2r, s3s, s3r, qs, qr, tzs, tzr, tds, tdr, m1s, m1r, m2s, m2r,
):
    dp, z = lax.axis_index("dp"), lax.axis_index("seq")
    x, y = dp % 2, dp // 2
    first, second = (x, y), (y, x)
    over_x, over_y = y * 2 + (1 - x), (1 - y) * 2 + x
    hop1, hop2 = (over_x, over_y), (over_y, over_x)
    others = (over_x, over_y, (1 - y) * 2 + (1 - x))
    ahead = [(z + e) % 4 for e in (1, 2, 3)]
    piece = [4 * h + 2 * first[h] + second[h] for h in range(2)]
    sent = []

    def send(src, dst, send_sem, recv_sem, target):
        copy = pltpu.make_async_remote_copy(
            src_ref=src, dst_ref=dst, send_sem=send_sem, recv_sem=recv_sem,
            device_id=target, device_id_type=pl.DeviceIdType.MESH,
        )
        copy.start()
        sent.append(copy)
        return copy

    barrier = pltpu.get_barrier_semaphore()
    for other in others:
        pl.semaphore_signal(
            barrier, inc=1, device_id={"dp": other}, device_id_type=pl.DeviceIdType.MESH
        )
    for other in ahead:
        pl.semaphore_signal(
            barrier, inc=1, device_id={"seq": other}, device_id_type=pl.DeviceIdType.MESH
        )
    pl.semaphore_wait(barrier, 6)

    block = ahead + [z]

    def start1(n):
        return [
            send(
                u.at[block[n], pl.ds(4 * h + 2 * (1 - first[h]), 2)], r1.at[h, n],
                s1s.at[h, n], s1r.at[h, n], {"dp": hop1[h]},
            )
            for h in range(2)
        ]

    small1 = [
        send(small, sb1.at[dp], m1s.at[d], m1r.at[d], {"dp": others[d]}) for d in range(3)
    ]
    sb1[dp] = small[...]
    stage1 = {0: start1(0), 1: start1(1)}
    stage2 = {}
    stage3 = []
    own = None

    def finish2(n):
        parts = []
        for h in range(2):
            stage2[n][h].wait_recv()
            parts.append(
                u[block[n], piece[h]].astype(F32)
                + r1[h, n, second[h]].astype(F32)
                + r2[h, n].astype(F32)
            )
        return parts

    def start3(n):
        parts = finish2(n)
        for h in range(2):
            a2[n, h] = parts[h].astype(BF16)
        stage3.append(send(a2.at[n], r3.at[n], s3s.at[n], s3r.at[n], {"seq": ahead[n]}))

    for n in range(4):
        copies = []
        for h in range(2):
            stage1[n][h].wait_recv()
            away = 1 - second[h]
            a1[h, n] = (
                u[block[n], 4 * h + 2 * first[h] + away].astype(F32)
                + r1[h, n, away].astype(F32)
            ).astype(BF16)
            copies.append(
                send(a1.at[h, n], r2.at[h, n], s2s.at[h, n], s2r.at[h, n], {"dp": hop2[h]})
            )
        stage2[n] = copies
        if n + 2 < 4:
            stage1[n + 2] = start1(n + 2)
        if n >= 1:
            start3(n - 1)
        if n == 0:
            for copy in small1:
                copy.wait_recv()
            sb2[z] = sb1[0] + sb1[1] + sb1[2] + sb1[3]
            small2 = [
                send(sb2.at[z], sb2.at[z], m2s.at[e], m2r.at[e], {"seq": ahead[e]})
                for e in range(3)
            ]
    own = finish2(3)
    for copy in stage3:
        copy.wait_recv()
    for h in range(2):
        total = own[h]
        for e in range(3):
            total = total + r3[e, h].astype(F32)
        total = total.astype(BF16)
        outq[piece[h]] = total[0:128]
        outt[piece[h], z] = total[128:160]
    table_z = [
        send(
            outt.at[piece[h], z], outt.at[piece[h], z], tzs.at[e, h], tzr.at[e, h],
            {"seq": ahead[e]},
        )
        for e in range(3)
        for h in range(2)
    ]
    last = [
        send(outq.at[piece[h]], outq.at[piece[h]], qs.at[d, h], qr.at[d, h], {"dp": others[d]})
        for d in range(3)
        for h in range(2)
    ]
    for copy in small2:
        copy.wait_recv()
    outs[...] = sb2[0] + sb2[1] + sb2[2] + sb2[3]
    for copy in table_z:
        copy.wait_recv()
    last += [
        send(outt.at[piece[h]], outt.at[piece[h]], tds.at[d, h], tdr.at[d, h], {"dp": others[d]})
        for d in range(3)
        for h in range(2)
    ]
    for copy in last:
        copy.wait_recv()
    for copy in sent:
        copy.wait_send()


def body(
    byte_ids, pad_lengths, table, conv_weight, score_weight, norm_gain, query_weight, query_grad
):
    ids = byte_ids[0]
    count = ids.shape[0]
    rows = count // 2
    vocab, chans = table.shape
    width = query_grad.shape[2]
    n_seq = lax.axis_size("seq")
    total = count * n_seq
    start = lax.axis_index("seq") * count
    limit = total - pad_lengths[0]
    ends = n_seq - 1
    up = [(i, i + 1) for i in range(ends)]
    down = [(i + 1, i) for i in range(ends)]
    ids_ext = jnp.concatenate(
        [lax.ppermute(ids[count - 3 :], "seq", up), ids, lax.ppermute(ids[:3], "seq", down)]
    )
    pos_e = start + jnp.arange(-3, count + 3, dtype=jnp.int32)
    ids_ext = jnp.where((pos_e >= 0) & (pos_e < limit), ids_ext, -1)
    halves = ids_ext.reshape(rows + 3, 2).T
    idm = jnp.stack([halves[j % 2, j // 2 : j // 2 + rows] for j in range(8)])
    pos = jnp.stack([start, limit, jnp.full_like(start, total)]).astype(jnp.int32)

    part = jnp.dot(
        conv_weight * score_weight, table.astype(F32).T, precision=lax.Precision.HIGHEST
    )
    p = jnp.pad(lax.psum(part, "tensor"), ((0, 5), (0, 0)))

    vm = pl.BlockSpec(memory_space=pltpu.VMEM)
    sm = pl.BlockSpec(memory_space=pltpu.SMEM)
    sw = score_weight[None, :]
    gain = norm_gain[None, :]
    pooled, ng, wt, sums, probs, grads = pl.pallas_call(
        forward_kernel,
        out_shape=(
            jax.ShapeDtypeStruct((rows, chans), F32),
            jax.ShapeDtypeStruct((rows, chans), F32),
            jax.ShapeDtypeStruct((3, vocab, rows), BF16),
            jax.ShapeDtypeStruct((16, rows), F32),
            jax.ShapeDtypeStruct((8, rows), F32),
            jax.ShapeDtypeStruct((rows, width), BF16),
        ),
        in_specs=[sm] + [vm] * 7,
        out_specs=(vm,) * 6,
        scratch_shapes=[
            pltpu.VMEM((3, rows, vocab), BF16),
            pltpu.VMEM((3, rows, vocab), BF16),
            pltpu.VMEM((3, vocab, rows), F32),
            pltpu.VMEM((3, vocab, rows), F32),
            pltpu.VMEM((rows, 128), F32),
            pltpu.VMEM((rows, 128), F32),
        ],
        name="forward",
    )(pos, idm, p, table, conv_weight, gain, query_weight, query_grad[0])
    sums = lax.psum(sums, "tensor")
    packed = (n_seq, lax.axis_size("dp"), chans, width, vocab) == (4, 4, 1024, 1024, 256)
    small_shape = jax.ShapeDtypeStruct((8, chans), F32)
    if packed:
        shapes = (jax.ShapeDtypeStruct((4, 8, 160, 256), BF16), small_shape)
    else:
        shapes = (
            jax.ShapeDtypeStruct((chans, width), BF16),
            jax.ShapeDtypeStruct((vocab, chans), BF16),
            small_shape,
        )
    shares = pl.pallas_call(
        backward_kernel,
        out_shape=shapes,
        in_specs=[sm] + [vm] * 11,
        out_specs=(vm,) * len(shapes),
        name="backward",
    )(pos, idm, sums, probs, table, conv_weight, sw, gain, pooled, ng, wt, grads)
    if not packed:
        share = lax.psum_scatter(shares[0], "seq", scatter_dimension=1, tiled=True)
        query_out = lax.psum(share, "dp")
        tab_out = lax.psum(shares[1], ("dp", "seq"))
        small_out = lax.psum(shares[2], ("dp", "seq"))
        return (tab_out, small_out[0:3], small_out[3], small_out[4], query_out)
    dma = pltpu.SemaphoreType.DMA
    outq, outt, outs = pl.pallas_call(
        reduce_kernel,
        out_shape=(
            jax.ShapeDtypeStruct((8, 128, 256), BF16),
            jax.ShapeDtypeStruct((8, 4, 32, 256), BF16),
            small_shape,
        ),
        in_specs=[vm] * 2,
        out_specs=(vm,) * 3,
        scratch_shapes=[
            pltpu.VMEM((2, 4, 2, 160, 256), BF16),
            pltpu.VMEM((2, 4, 160, 256), BF16),
            pltpu.VMEM((2, 4, 160, 256), BF16),
            pltpu.VMEM((3, 2, 160, 256), BF16),
            pltpu.VMEM((3, 2, 160, 256), BF16),
            pltpu.VMEM((4, 8, chans), F32),
            pltpu.VMEM((4, 8, chans), F32),
        ]
        + [dma((2, 4))] * 4
        + [dma((3,))] * 2
        + [dma((3, 2))] * 6
        + [dma((3,))] * 4,
        compiler_params=pltpu.CompilerParams(collective_id=0, has_side_effects=True),
        name="reduce",
    )(*shares)
    tab_out = outt.transpose(0, 2, 1, 3).reshape(vocab, chans)
    return (tab_out, outs[0:3], outs[3], outs[4], outq.reshape(chans, width // n_seq))


def solution(mesh):
    return jax.shard_map(
        body,
        mesh=mesh,
        in_specs=(
            P("dp", "seq"),
            P("dp"),
            P(None, "tensor"),
            P(None, "tensor"),
            P("tensor"),
            P("tensor"),
            P("tensor", None),
            P("dp", "seq", None),
        ),
        out_specs=(
            P(None, "tensor"),
            P(None, "tensor"),
            P("tensor"),
            P("tensor"),
            P("tensor", "seq"),
        ),
        check_vma=False,
    )
```

```python
import functools

import jax
import jax.numpy as jnp
from jax import lax
from jax.experimental import pallas as pl
from jax.experimental.pallas import tpu as pltpu
from jax.sharding import PartitionSpec as P

D = 2048
EPS = 1e-06
F32 = jnp.float32
BF16 = jnp.bfloat16
OFFS = range(-2, 4)
CHUNK = 256

NN = (((1,), (0,)), ((), ()))
NT = (((1,), (1,)), ((), ()))
TN = (((0,), (0,)), ((), ()))


def mm(lhs, rhs, dims):
    return lax.dot_general(lhs, rhs, dims, preferred_element_type=F32)


def block_weights(start, total, rows):
    i = lax.broadcasted_iota(jnp.int32, (1, rows), 1)
    even = (i % 2) == 0
    inside = {o: (start + 2 * i + o >= 0) & (start + 2 * i + o < total) for o in OFFS}
    table = []
    for b in range(4):
        for p in range(2):
            row = {}
            for o in OFFS:
                if b == 0:
                    if o == p:
                        row[o] = jnp.where(inside[o], 1.0, 0.0)
                elif b == 1:
                    if o in (0, 1):
                        row[o] = jnp.where(inside[o], 0.5, 0.0)
                elif b == 3:
                    if o in (0, 1):
                        row[o] = jnp.where(inside[o], 0.25, 0.0)
                    else:
                        row[o] = jnp.where(inside[o] & (even if o > 1 else ~even), 0.25, 0.0)
                else:
                    d = o - p
                    if -2 <= d <= 2:
                        r = (start + 2 * i + p) % 3
                        row[o] = jnp.where(inside[o] & (r >= -d) & (r <= 2 - d), 1.0 / 3.0, 0.0)
            table.append(row)
    return table


def spread(idm, rows_of, tap):
    rows = idm.shape[1]
    v = lax.broadcasted_iota(jnp.int32, (256, rows), 0)
    acc = None
    for o in OFFS:
        at = o + tap + 2
        term = jnp.where(idm[at : at + 1, :] == v, rows_of[o], 0.0)
        acc = term if acc is None else acc + term
    return acc


def send_to(sent, src, dst, send_sem, recv_sem, target):
    copy = pltpu.make_async_remote_copy(
        src_ref=src, dst_ref=dst, send_sem=send_sem, recv_sem=recv_sem,
        device_id=target, device_id_type=pl.DeviceIdType.MESH,
    )
    copy.start()
    sent.append(copy)
    return copy


def greet(target):
    pl.semaphore_signal(
        pltpu.get_barrier_semaphore(), inc=1, device_id=target,
        device_id_type=pl.DeviceIdType.MESH,
    )


def split3(value):
    hi = value.astype(BF16)
    rest = value - hi.astype(F32)
    mid = rest.astype(BF16)
    low = (rest - mid.astype(F32)).astype(BF16)
    parts = [hi.astype(F32), mid.astype(F32), low.astype(F32)]
    return jnp.concatenate(parts, axis=0).astype(BF16)


def shifted(own, before, after, by):
    if by == 0:
        return own
    rows = own.shape[1]
    i = lax.broadcasted_iota(jnp.int32, own.shape, 1)
    turn = (-by) % rows
    side = after if by > 0 else before
    outside = (i + by >= rows) if by > 0 else (i + by < 0)
    return jnp.where(outside, pltpu.roll(side, turn, 1), pltpu.roll(own, turn, 1))


def forward(
    start, limit, total, halo, sent, ids_ref, table_ref, cw_ref, sw_ref, gain_ref, wq_ref, g_ref,
    pooled_ref, ng_ref, wt_ref, grads_ref, pbuf, sums_buf,
    wh, wl, r1, r2, sq, rd, psend, precv, ssend, srecv, other_core,
):
    rows = ids_ref.shape[1]
    chans = table_ref.shape[1]
    part = None
    six = split3(
        jnp.concatenate([cw_ref[...] * sw_ref[...], jnp.zeros((5, chans), F32)], axis=0)
    )
    part = mm(six, table_ref[...], NT)
    pbuf[0] = part[0:8] + part[8:16] + part[16:24]
    exchange = send_to(sent, pbuf.at[0], pbuf.at[1], psend, precv, other_core)
    keep = (start + 2 * lax.broadcasted_iota(jnp.int32, g_ref.shape, 0)) < limit
    grads_ref[...] = jnp.where(keep, g_ref[...].astype(F32), 0.0).astype(BF16)
    r1[...] = jnp.zeros_like(r1)
    r2[...] = jnp.zeros_like(r2)
    sq[...] = jnp.zeros_like(sq)
    rd[...] = jnp.zeros_like(rd)
    i = lax.broadcasted_iota(jnp.int32, (1, rows), 1)
    v = lax.broadcasted_iota(jnp.int32, (256, rows), 0)
    before, after = halo()
    own = ids_ref[...]
    lines = []
    for at in range(8):
        j = at - 3
        n, by = j % 2, j // 2
        line = shifted(own[n : n + 1], before[n : n + 1], after[n : n + 1], by)
        byte = start + 2 * i + j
        lines.append(jnp.where((byte >= 0) & (byte < limit), line, -1))
    idm = jnp.concatenate(lines, axis=0)
    exchange.wait_recv()
    p3 = split3(pbuf[0] + pbuf[1])
    picks = []
    for j in range(8):
        hot = jnp.where(idm[j : j + 1, :] == v, 1.0, 0.0).astype(BF16)
        g = mm(p3, hot, NN)
        picks.append(g[0:8] + g[8:16] + g[16:24])
    s = {o: picks[o + 2][0:1] + picks[o + 3][1:2] + picks[o + 4][2:3] for o in OFFS}
    weights = block_weights(start, total, rows)
    expo = []
    for row in weights:
        score = None
        for o in row:
            score = row[o] * s[o] if score is None else score + row[o] * s[o]
        expo.append(jnp.exp(score))
    probs = []
    for n in range(8):
        whole = expo[n % 2] + expo[2 + n % 2] + expo[4 + n % 2] + expo[6 + n % 2]
        probs.append(expo[n] / whole)
    a = {}
    for o in OFFS:
        acc = None
        for n in range(8):
            if o in weights[n]:
                term = probs[n] * weights[n][o]
                acc = term if acc is None else acc + term
        a[o] = 0.5 * acc
    for k in range(3):
        w = spread(idm, a, k)
        wt_ref[k] = w.astype(BF16)
        wf = w.T
        top = wf.astype(BF16)
        wh[k] = top
        wl[k] = (wf - top.astype(F32)).astype(BF16)

    def step(c, carry):
        at = pl.ds(pl.multiple_of(c * CHUNK, CHUNK), CHUNK)
        tab = table_ref[:, at]
        cw = cw_ref[:, at]
        ng = mm(grads_ref[...], wq_ref[at, :], NT)
        pooled = None
        for k in range(3):
            part = cw[k : k + 1] * (mm(wh[k], tab, NN) + mm(wl[k], tab, NN))
            pooled = part if pooled is None else pooled + part
        pooled_ref[:, at] = pooled
        ng_ref[:, at] = ng
        gained = ng * gain_ref[:, at]
        square = pooled * pooled
        inner = pooled * gained
        sq[...] += square[:, 0:128] + square[:, 128:256]
        rd[...] += inner[:, 0:128] + inner[:, 128:256]
        gb = gained.astype(BF16)
        pb = pooled.astype(BF16)
        for k in range(3):
            tk = (tab.astype(F32) * cw[k : k + 1]).astype(BF16)
            r1[k] += mm(tk, gb, NT)
            r2[k] += mm(tk, pb, NT)
        return carry

    lax.fori_loop(0, chans // CHUNK, step, 0)
    out = []
    for r in (r1, r2):
        for o in OFFS:
            acc = None
            for k in range(3):
                at = o + k + 2
                term = jnp.where(idm[at : at + 1, :] == v, r[k], 0.0)
                acc = term if acc is None else acc + term
            out.append(jnp.sum(acc, axis=0, keepdims=True))
    out.append(jnp.sum(sq[...].T, axis=0, keepdims=True))
    out.append(jnp.sum(rd[...].T, axis=0, keepdims=True))
    out.append(jnp.zeros((2, rows), F32))
    sums_buf[0] = jnp.concatenate(out, axis=0)
    exchange = send_to(sent, sums_buf.at[0], sums_buf.at[1], ssend, srecv, other_core)
    return idm, probs, weights, exchange


def table_terms(
    idm, probs, weights, sums, scale, pull, scale_c, pull_c, table_ref, cw_ref, sw_ref, gain_ref,
    pooled_ref, ng_ref, wt_ref, put, small_ref,
):
    chans = table_ref.shape[1]
    q = {o: scale * sums[o + 2 : o + 3] - pull * sums[o + 8 : o + 9] for o in OFFS}
    pgrad = []
    for row in weights:
        acc = None
        for o in row:
            acc = row[o] * q[o] if acc is None else acc + row[o] * q[o]
        pgrad.append(0.5 * acc)
    sgrad = []
    for n in range(8):
        mean = None
        for m in range(n % 2, 8, 2):
            term = probs[m] * pgrad[m]
            mean = term if mean is None else mean + term
        sgrad.append(probs[n] * (pgrad[n] - mean))
    ds = {}
    for o in OFFS:
        acc = None
        for n in range(8):
            if o in weights[n]:
                term = sgrad[n] * weights[n][o]
                acc = term if acc is None else acc + term
        ds[o] = acc
    hist = [jnp.sum(spread(idm, ds, k), axis=1, keepdims=True) for k in range(3)]
    for c in range(chans // CHUNK):
        at = pl.ds(c * CHUNK, CHUNK)
        tab = table_ref[:, at].astype(F32)
        cw = cw_ref[:, at]
        sw = sw_ref[:, at]
        ng = ng_ref[:, at]
        pooled = pooled_ref[:, at]
        gain_term = jnp.sum(ng * pooled * scale_c, axis=0, keepdims=True)
        pg = (ng * gain_ref[:, at] * scale_c - pull_c * pooled).astype(BF16)
        total_t = None
        outs = []
        score = None
        for k in range(3):
            full = mm(wt_ref[k], pg, NN) + hist[k] * sw
            term = cw[k : k + 1] * full
            total_t = term if total_t is None else total_t + term
            outs.append(jnp.sum(full * tab, axis=0, keepdims=True))
            term = cw[k : k + 1] * jnp.sum(hist[k] * tab, axis=0, keepdims=True)
            score = term if score is None else score + term
        put(c, total_t.astype(BF16))
        small_ref[:, at] = jnp.concatenate(
            outs + [score, gain_term, jnp.zeros((3, CHUNK), F32)], axis=0
        )


def kernel(
    packed, n_seq, *refs,
):
    pos_ref, ids_ref, table_ref, cw_ref, sw_ref, gain_ref, wq_ref, g_ref = refs[:8]
    outs3 = refs[8:11]
    (
        pooled_ref, ng_ref, wt_ref, grads_ref, pbuf, sums_buf, wh, wl, r1, r2, sq, rd,
        before_ref, after_ref, normed, core_s, core_r, halo_s, halo_r,
    ) = refs[11:30]
    sent = []
    dp, z, core = lax.axis_index("dp"), lax.axis_index("seq"), lax.axis_index("tensor")
    x, y = dp % 2, dp // 2
    over_x, over_y = y * 2 + (1 - x), (1 - y) * 2 + x
    others = (over_x, over_y, (1 - y) * 2 + (1 - x))
    reach = range(1, 4) if packed else (1, n_seq - 1)
    ahead = [(z + e) % n_seq for e in reach]
    other_core = {"tensor": 1 - core}
    barrier = pltpu.get_barrier_semaphore()
    greet(other_core)
    for there in ahead:
        greet({"seq": there})
    if packed:
        for there in others:
            greet({"dp": there})
    pl.semaphore_wait(barrier, 1 + len(ahead) + (3 if packed else 0))
    halos = [
        send_to(sent, ids_ref, before_ref, halo_s.at[0], halo_r.at[0], {"seq": ahead[0]}),
        send_to(sent, ids_ref, after_ref, halo_s.at[1], halo_r.at[1], {"seq": ahead[-1]}),
    ]

    def halo():
        for copy in halos:
            copy.wait_recv()
        return before_ref[...], after_ref[...]

    rows = ids_ref.shape[1]
    chans = table_ref.shape[1]
    start, limit, total = z * (2 * rows), pos_ref[0], n_seq * 2 * rows
    idm, probs, weights, exchange = forward(
        start, limit, total, halo, sent, ids_ref, table_ref, cw_ref, sw_ref, gain_ref, wq_ref,
        g_ref, pooled_ref, ng_ref, wt_ref, grads_ref, pbuf, sums_buf, wh, wl, r1, r2, sq, rd,
        core_s.at[0], core_r.at[0], core_s.at[1], core_r.at[1], other_core,
    )
    exchange.wait_recv()
    sums = sums_buf[0] + sums_buf[1]
    scale = lax.rsqrt(sums[12:13] / D + EPS)
    pull = scale * scale * scale * (sums[13:14] / D)
    cols = jnp.concatenate([scale, pull, jnp.zeros((6, rows), F32)], axis=0).T
    scale_c, pull_c = cols[:, 0:1], cols[:, 1:2]
    normed[...] = (pooled_ref[...] * scale_c * gain_ref[...]).astype(BF16)

    def tables(put, small_ref):
        table_terms(
            idm, probs, weights, sums, scale, pull, scale_c, pull_c, table_ref, cw_ref, sw_ref,
            gain_ref, pooled_ref, ng_ref, wt_ref, put, small_ref,
        )

    if not packed:
        query_ref, tab_ref, small_ref = outs3

        def put(c, value):
            tab_ref[:, pl.ds(c * CHUNK, CHUNK)] = value

        for c in range(chans // CHUNK):
            at = pl.ds(c * CHUNK, CHUNK)
            query_ref[at, :] = mm(normed[:, at], grads_ref[...], TN).astype(BF16)
        tables(put, small_ref)
        for copy in sent:
            copy.wait_send()
        return

    tab_out, small_out, query_out = outs3
    (
        uq, ut, small, q1, qa1, q2, qa2, q3, t1, ta1, t2, ta2, t3, outq, outt, sb1, sb2,
        s1s, s1r, s2s, s2r, s3s, s3r, qs, qr, tzs, tzr, tds, tdr, m1s, m1r, m2s, m2r,
        u1s, u1r, u2s, u2r, u3s, u3r,
    ) = refs[30:]
    send = functools.partial(send_to, sent)
    first, second = (x, y), (y, x)
    hop1, hop2 = (over_x, over_y), (over_y, over_x)
    piece = [4 * h + 2 * first[h] + second[h] for h in range(2)]
    give1 = [pl.ds(4 * h + 2 * (1 - first[h]), 2) for h in range(2)]
    give2 = [4 * h + 2 * first[h] + 1 - second[h] for h in range(2)]
    block = ahead + [z]

    def query_block(n):
        at = pl.ds(pl.multiple_of(block[n] * 256, 256), 256)
        value = mm(normed[...], grads_ref[:, at], TN).astype(BF16)
        for m in range(8):
            uq[block[n], m] = value[128 * m : 128 * m + 128]
        return [
            send(
                uq.at[block[n], give1[h]], q1.at[h, n], s1s.at[h, n], s1r.at[h, n],
                {"dp": hop1[h]},
            )
            for h in range(2)
        ]

    def put(c, value):
        for m in range(8):
            ut[m, c] = value[32 * m : 32 * m + 32]

    stage1 = {n: query_block(n) for n in (0, 1)}
    tables(put, small)
    small1 = [
        send(small, sb1.at[dp], m1s.at[d], m1r.at[d], {"dp": others[d]}) for d in range(3)
    ]
    sb1[dp] = small[...]
    tab1 = [
        send(ut.at[give1[h]], t1.at[h], u1s.at[h], u1r.at[h], {"dp": hop1[h]}) for h in range(2)
    ]
    for n in (2, 3):
        stage1[n] = query_block(n)
    stage2 = {}
    stage3 = []

    def relay(n):
        copies = []
        for h in range(2):
            stage1[n][h].wait_recv()
            qa1[h, n] = (
                uq[block[n], give2[h]].astype(F32) + q1[h, n, 1 - second[h]].astype(F32)
            ).astype(BF16)
            copies.append(
                send(qa1.at[h, n], q2.at[h, n], s2s.at[h, n], s2r.at[h, n], {"dp": hop2[h]})
            )
        stage2[n] = copies

    def gathered(n):
        parts = []
        for h in range(2):
            stage2[n][h].wait_recv()
            parts.append(
                uq[block[n], piece[h]].astype(F32)
                + q1[h, n, second[h]].astype(F32)
                + q2[h, n].astype(F32)
            )
        return parts

    def pass_on(n):
        parts = gathered(n)
        for h in range(2):
            qa2[n, h] = parts[h].astype(BF16)
        stage3.append(send(qa2.at[n], q3.at[n], s3s.at[n], s3r.at[n], {"seq": ahead[n]}))

    relay(0)
    relay(1)
    pass_on(0)
    tab2 = []
    for h in range(2):
        tab1[h].wait_recv()
        ta1[h] = (ut[give2[h]].astype(F32) + t1[h, 1 - second[h]].astype(F32)).astype(BF16)
        tab2.append(send(ta1.at[h], t2.at[h], u2s.at[h], u2r.at[h], {"dp": hop2[h]}))
    for copy in small1:
        copy.wait_recv()
    sb2[z] = sb1[0] + sb1[1] + sb1[2] + sb1[3]
    small2 = [
        send(sb2.at[z], sb2.at[z], m2s.at[e], m2r.at[e], {"seq": ahead[e]}) for e in range(3)
    ]
    pass_on(1)
    relay(2)
    for h in range(2):
        tab2[h].wait_recv()
        value = ut[piece[h]].astype(F32) + t1[h, second[h]].astype(F32) + t2[h].astype(F32)
        for zb in range(4):
            ta2[zb, h] = value[zb].astype(BF16)
    tab3 = [
        send(ta2.at[ahead[e]], t3.at[e], u3s.at[e], u3r.at[e], {"seq": ahead[e]})
        for e in range(3)
    ]
    relay(3)
    pass_on(2)
    for copy in tab3:
        copy.wait_recv()
    for h in range(2):
        value = ta2[z, h].astype(F32)
        for e in range(3):
            value = value + t3[e, h].astype(F32)
        outt[piece[h], z] = value.astype(BF16)
    table_z = [
        send(
            outt.at[piece[h], z], outt.at[piece[h], z], tzs.at[e, h], tzr.at[e, h],
            {"seq": ahead[e]},
        )
        for e in range(3)
        for h in range(2)
    ]
    own = gathered(3)
    for copy in stage3:
        copy.wait_recv()
    for h in range(2):
        value = own[h]
        for e in range(3):
            value = value + q3[e, h].astype(F32)
        outq[piece[h]] = value.astype(BF16)
    last = [
        send(outq.at[piece[h]], outq.at[piece[h]], qs.at[d, h], qr.at[d, h], {"dp": others[d]})
        for d in range(3)
        for h in range(2)
    ]
    for copy in table_z:
        copy.wait_recv()
    last_t = [
        send(outt.at[piece[h]], outt.at[piece[h]], tds.at[d, h], tdr.at[d, h], {"dp": others[d]})
        for d in range(3)
        for h in range(2)
    ]
    for copy in small2:
        copy.wait_recv()
    small_out[...] = sb2[0] + sb2[1] + sb2[2] + sb2[3]
    for copy in last:
        copy.wait_recv()
    for m in range(8):
        query_out[128 * m : 128 * m + 128, :] = outq[m]
    for copy in last_t:
        copy.wait_recv()
    for m in range(8):
        for zb in range(4):
            tab_out[32 * m : 32 * m + 32, 256 * zb : 256 * zb + 256] = outt[m, zb]
    for copy in sent:
        copy.wait_send()


def body(
    byte_ids, pad_lengths, table, conv_weight, score_weight, norm_gain, query_weight, query_grad
):
    count = byte_ids.shape[1]
    rows = count // 2
    vocab, chans = table.shape
    width = query_grad.shape[2]
    n_seq = lax.axis_size("seq")
    limit = count * n_seq - pad_lengths
    halves = byte_ids.reshape(rows, 2).T
    packed = (n_seq, lax.axis_size("dp"), chans, width, vocab) == (4, 4, 1024, 1024, 256)
    vm = pl.BlockSpec(memory_space=pltpu.VMEM)
    sm = pl.BlockSpec(memory_space=pltpu.SMEM)
    dma = pltpu.SemaphoreType.DMA
    small_shape = jax.ShapeDtypeStruct((8, chans), F32)
    tab_shape = jax.ShapeDtypeStruct((vocab, chans), BF16)
    if packed:
        shapes = (tab_shape, small_shape, jax.ShapeDtypeStruct((chans, width // 4), BF16))
    else:
        shapes = (jax.ShapeDtypeStruct((chans, width), BF16), tab_shape, small_shape)
    scratch = [
        pltpu.VMEM((rows, chans), F32),
        pltpu.VMEM((rows, chans), F32),
        pltpu.VMEM((3, vocab, rows), BF16),
        pltpu.VMEM((rows, width), BF16),
        pltpu.VMEM((2, 8, vocab), F32),
        pltpu.VMEM((2, 16, rows), F32),
        pltpu.VMEM((3, rows, vocab), BF16),
        pltpu.VMEM((3, rows, vocab), BF16),
        pltpu.VMEM((3, vocab, rows), F32),
        pltpu.VMEM((3, vocab, rows), F32),
        pltpu.VMEM((rows, 128), F32),
        pltpu.VMEM((rows, 128), F32),
        pltpu.VMEM((2, rows), jnp.int32),
        pltpu.VMEM((2, rows), jnp.int32),
        pltpu.VMEM((rows, chans), BF16),
    ] + [dma((2,))] * 4
    if packed:
        scratch += [
            pltpu.VMEM((4, 8, 128, 256), BF16),
            pltpu.VMEM((8, 4, 32, 256), BF16),
            pltpu.VMEM((8, chans), F32),
            pltpu.VMEM((2, 4, 2, 128, 256), BF16),
            pltpu.VMEM((2, 4, 128, 256), BF16),
            pltpu.VMEM((2, 4, 128, 256), BF16),
            pltpu.VMEM((3, 2, 128, 256), BF16),
            pltpu.VMEM((3, 2, 128, 256), BF16),
            pltpu.VMEM((2, 2, 4, 32, 256), BF16),
            pltpu.VMEM((2, 4, 32, 256), BF16),
            pltpu.VMEM((2, 4, 32, 256), BF16),
            pltpu.VMEM((4, 2, 32, 256), BF16),
            pltpu.VMEM((3, 2, 32, 256), BF16),
            pltpu.VMEM((8, 128, 256), BF16),
            pltpu.VMEM((8, 4, 32, 256), BF16),
            pltpu.VMEM((4, 8, chans), F32),
            pltpu.VMEM((4, 8, chans), F32),
        ]
        scratch += (
            [dma((2, 4))] * 4 + [dma((3,))] * 2 + [dma((3, 2))] * 6 + [dma((3,))] * 4
            + [dma((2,))] * 4 + [dma((3,))] * 2
        )
    results = pl.pallas_call(
        functools.partial(kernel, packed, n_seq),
        out_shape=shapes,
        in_specs=[sm] + [vm] * 7,
        out_specs=(vm,) * 3,
        scratch_shapes=scratch,
        compiler_params=pltpu.CompilerParams(collective_id=0, has_side_effects=True),
        name="tokenizer_backward",
    )(
        limit, halves, table, conv_weight, score_weight[None, :], norm_gain[None, :],
        query_weight, query_grad[0],
    )
    if packed:
        tab_out, small_out, query_out = results
    else:
        share = lax.psum_scatter(results[0], "seq", scatter_dimension=1, tiled=True)
        query_out = lax.psum(share, "dp")
        tab_out = lax.psum(results[1], ("dp", "seq"))
        small_out = lax.psum(results[2], ("dp", "seq"))
    return (tab_out, small_out[0:3], small_out[3], small_out[4], query_out)


def solution(mesh):
    return jax.shard_map(
        body,
        mesh=mesh,
        in_specs=(
            P("dp", "seq"),
            P("dp"),
            P(None, "tensor"),
            P(None, "tensor"),
            P("tensor"),
            P("tensor"),
            P("tensor", None),
            P("dp", "seq", None),
        ),
        out_specs=(
            P(None, "tensor"),
            P(None, "tensor"),
            P("tensor"),
            P("tensor"),
            P("tensor", "seq"),
        ),
        check_vma=False,
    )
```

```python
import functools

import jax
import jax.numpy as jnp
from jax import lax
from jax.experimental import pallas as pl
from jax.experimental.pallas import tpu as pltpu
from jax.sharding import PartitionSpec as P

D = 2048
EPS = 1e-06
F32 = jnp.float32
BF16 = jnp.bfloat16
OFFS = range(-2, 4)
CHUNK = 256

NN = (((1,), (0,)), ((), ()))
NT = (((1,), (1,)), ((), ()))
TN = (((0,), (0,)), ((), ()))


def mm(lhs, rhs, dims):
    return lax.dot_general(lhs, rhs, dims, preferred_element_type=F32)


def block_weights(start, total, rows):
    i = lax.broadcasted_iota(jnp.int32, (1, rows), 1)
    even = (i % 2) == 0
    inside = {o: (start + 2 * i + o >= 0) & (start + 2 * i + o < total) for o in OFFS}
    table = []
    for b in range(4):
        for p in range(2):
            row = {}
            for o in OFFS:
                if b == 0:
                    if o == p:
                        row[o] = jnp.where(inside[o], 1.0, 0.0)
                elif b == 1:
                    if o in (0, 1):
                        row[o] = jnp.where(inside[o], 0.5, 0.0)
                elif b == 3:
                    if o in (0, 1):
                        row[o] = jnp.where(inside[o], 0.25, 0.0)
                    else:
                        row[o] = jnp.where(inside[o] & (even if o > 1 else ~even), 0.25, 0.0)
                else:
                    d = o - p
                    if -2 <= d <= 2:
                        r = (start + 2 * i + p) % 3
                        row[o] = jnp.where(inside[o] & (r >= -d) & (r <= 2 - d), 1.0 / 3.0, 0.0)
            table.append(row)
    return table


def spread(idm, rows_of, tap):
    rows = idm.shape[1]
    v = lax.broadcasted_iota(jnp.int32, (256, rows), 0)
    acc = None
    for o in OFFS:
        at = o + tap + 2
        term = jnp.where(idm[at : at + 1, :] == v, rows_of[o], 0.0)
        acc = term if acc is None else acc + term
    return acc


def send_to(sent, src, dst, send_sem, recv_sem, target):
    copy = pltpu.make_async_remote_copy(
        src_ref=src, dst_ref=dst, send_sem=send_sem, recv_sem=recv_sem,
        device_id=target, device_id_type=pl.DeviceIdType.MESH,
    )
    copy.start()
    sent.append(copy)
    return copy


def greet(target):
    pl.semaphore_signal(
        pltpu.get_barrier_semaphore(), inc=1, device_id=target,
        device_id_type=pl.DeviceIdType.MESH,
    )


def split3(value):
    hi = value.astype(BF16)
    rest = value - hi.astype(F32)
    mid = rest.astype(BF16)
    low = (rest - mid.astype(F32)).astype(BF16)
    parts = [hi.astype(F32), mid.astype(F32), low.astype(F32)]
    return jnp.concatenate(parts, axis=0).astype(BF16)


def shifted(own, before, after, by):
    if by == 0:
        return own
    rows = own.shape[1]
    i = lax.broadcasted_iota(jnp.int32, own.shape, 1)
    turn = (-by) % rows
    side = after if by > 0 else before
    outside = (i + by >= rows) if by > 0 else (i + by < 0)
    return jnp.where(outside, pltpu.roll(side, turn, 1), pltpu.roll(own, turn, 1))


def forward(
    start, limit, total, halo, sent, ids_ref, table_ref, cw_ref, sw_ref, gain_ref, wq_ref, g_ref,
    pooled_ref, ng_ref, wt_ref, grads_ref, pbuf, sums_buf,
    wh, wl, r1, r2, sq, rd, psend, precv, ssend, srecv, other_core,
):
    rows = ids_ref.shape[1]
    chans = table_ref.shape[1]
    part = None
    six = split3(
        jnp.concatenate([cw_ref[...] * sw_ref[...], jnp.zeros((5, chans), F32)], axis=0)
    )
    part = mm(six, table_ref[...], NT)
    pbuf[0] = part[0:8] + part[8:16] + part[16:24]
    exchange = send_to(sent, pbuf.at[0], pbuf.at[1], psend, precv, other_core)
    keep = (start + 2 * lax.broadcasted_iota(jnp.int32, g_ref.shape, 0)) < limit
    grads_ref[...] = jnp.where(keep, g_ref[...].astype(F32), 0.0).astype(BF16)
    r1[...] = jnp.zeros_like(r1)
    r2[...] = jnp.zeros_like(r2)
    sq[...] = jnp.zeros_like(sq)
    rd[...] = jnp.zeros_like(rd)
    i = lax.broadcasted_iota(jnp.int32, (1, rows), 1)
    v = lax.broadcasted_iota(jnp.int32, (256, rows), 0)
    before, after = halo()
    own = ids_ref[...]
    lines = []
    for at in range(8):
        j = at - 3
        n, by = j % 2, j // 2
        line = shifted(own[n : n + 1], before[n : n + 1], after[n : n + 1], by)
        byte = start + 2 * i + j
        lines.append(jnp.where((byte >= 0) & (byte < limit), line, -1))
    idm = jnp.concatenate(lines, axis=0)
    exchange.wait_recv()
    p3 = split3(pbuf[0] + pbuf[1])
    picks = []
    for j in range(8):
        hot = jnp.where(idm[j : j + 1, :] == v, 1.0, 0.0).astype(BF16)
        g = mm(p3, hot, NN)
        picks.append(g[0:8] + g[8:16] + g[16:24])
    s = {o: picks[o + 2][0:1] + picks[o + 3][1:2] + picks[o + 4][2:3] for o in OFFS}
    weights = block_weights(start, total, rows)
    expo = []
    for row in weights:
        score = None
        for o in row:
            score = row[o] * s[o] if score is None else score + row[o] * s[o]
        expo.append(jnp.exp(score))
    probs = []
    for n in range(8):
        whole = expo[n % 2] + expo[2 + n % 2] + expo[4 + n % 2] + expo[6 + n % 2]
        probs.append(expo[n] / whole)
    a = {}
    for o in OFFS:
        acc = None
        for n in range(8):
            if o in weights[n]:
                term = probs[n] * weights[n][o]
                acc = term if acc is None else acc + term
        a[o] = 0.5 * acc
    for k in range(3):
        w = spread(idm, a, k)
        wt_ref[k] = w.astype(BF16)
        wf = w.T
        top = wf.astype(BF16)
        wh[k] = top
        wl[k] = (wf - top.astype(F32)).astype(BF16)

    def step(c, carry):
        at = pl.ds(pl.multiple_of(c * CHUNK, CHUNK), CHUNK)
        tab = table_ref[:, at]
        cw = cw_ref[:, at]
        ng = mm(grads_ref[...], wq_ref[at, :], NT)
        pooled = None
        for k in range(3):
            part = cw[k : k + 1] * (mm(wh[k], tab, NN) + mm(wl[k], tab, NN))
            pooled = part if pooled is None else pooled + part
        pooled_ref[:, at] = pooled
        ng_ref[:, at] = ng
        gained = ng * gain_ref[:, at]
        square = pooled * pooled
        inner = pooled * gained
        sq[...] += square[:, 0:128] + square[:, 128:256]
        rd[...] += inner[:, 0:128] + inner[:, 128:256]
        gb = gained.astype(BF16)
        pb = pooled.astype(BF16)
        for k in range(3):
            tk = (tab.astype(F32) * cw[k : k + 1]).astype(BF16)
            r1[k] += mm(tk, gb, NT)
            r2[k] += mm(tk, pb, NT)
        return carry

    lax.fori_loop(0, chans // CHUNK, step, 0)
    out = []
    for r in (r1, r2):
        for o in OFFS:
            acc = None
            for k in range(3):
                at = o + k + 2
                term = jnp.where(idm[at : at + 1, :] == v, r[k], 0.0)
                acc = term if acc is None else acc + term
            out.append(jnp.sum(acc, axis=0, keepdims=True))
    out.append(jnp.sum(sq[...].T, axis=0, keepdims=True))
    out.append(jnp.sum(rd[...].T, axis=0, keepdims=True))
    out.append(jnp.zeros((2, rows), F32))
    sums_buf[0] = jnp.concatenate(out, axis=0)
    exchange = send_to(sent, sums_buf.at[0], sums_buf.at[1], ssend, srecv, other_core)
    return idm, probs, weights, exchange


def table_terms(
    idm, probs, weights, sums, scale, pull, scale_c, pull_c, table_ref, cw_ref, sw_ref, gain_ref,
    pooled_ref, ng_ref, wt_ref, put, small_ref,
):
    chans = table_ref.shape[1]
    q = {o: scale * sums[o + 2 : o + 3] - pull * sums[o + 8 : o + 9] for o in OFFS}
    pgrad = []
    for row in weights:
        acc = None
        for o in row:
            acc = row[o] * q[o] if acc is None else acc + row[o] * q[o]
        pgrad.append(0.5 * acc)
    sgrad = []
    for n in range(8):
        mean = None
        for m in range(n % 2, 8, 2):
            term = probs[m] * pgrad[m]
            mean = term if mean is None else mean + term
        sgrad.append(probs[n] * (pgrad[n] - mean))
    ds = {}
    for o in OFFS:
        acc = None
        for n in range(8):
            if o in weights[n]:
                term = sgrad[n] * weights[n][o]
                acc = term if acc is None else acc + term
        ds[o] = acc
    hist = [jnp.sum(spread(idm, ds, k), axis=1, keepdims=True) for k in range(3)]
    for c in range(chans // CHUNK):
        at = pl.ds(c * CHUNK, CHUNK)
        tab = table_ref[:, at].astype(F32)
        cw = cw_ref[:, at]
        sw = sw_ref[:, at]
        ng = ng_ref[:, at]
        pooled = pooled_ref[:, at]
        gain_term = jnp.sum(ng * pooled * scale_c, axis=0, keepdims=True)
        pg = (ng * gain_ref[:, at] * scale_c - pull_c * pooled).astype(BF16)
        total_t = None
        outs = []
        score = None
        for k in range(3):
            full = mm(wt_ref[k], pg, NN) + hist[k] * sw
            term = cw[k : k + 1] * full
            total_t = term if total_t is None else total_t + term
            outs.append(jnp.sum(full * tab, axis=0, keepdims=True))
            term = cw[k : k + 1] * jnp.sum(hist[k] * tab, axis=0, keepdims=True)
            score = term if score is None else score + term
        put(c, total_t.astype(BF16))
        small_ref[:, at] = jnp.concatenate(
            outs + [score, gain_term, jnp.zeros((3, CHUNK), F32)], axis=0
        )


def kernel(
    packed, n_seq, *refs,
):
    pos_ref, ids_ref, table_ref, cw_ref, sw_ref, gain_ref, wq_ref, g_ref = refs[:8]
    outs3 = refs[8:11]
    (
        pooled_ref, ng_ref, wt_ref, grads_ref, pbuf, sums_buf, wh, wl, r1, r2, sq, rd,
        before_ref, after_ref, normed, core_s, core_r, halo_s, halo_r,
    ) = refs[11:30]
    sent = []
    dp, z, core = lax.axis_index("dp"), lax.axis_index("seq"), lax.axis_index("tensor")
    x, y = dp % 2, dp // 2
    over_x, over_y = y * 2 + (1 - x), (1 - y) * 2 + x
    others = (over_x, over_y, (1 - y) * 2 + (1 - x))
    reach = range(1, 4) if packed else (1, n_seq - 1)
    ahead = [(z + e) % n_seq for e in reach]
    other_core = {"tensor": 1 - core}
    barrier = pltpu.get_barrier_semaphore()
    greet(other_core)
    for there in ahead:
        greet({"seq": there})
    if packed:
        for there in others:
            greet({"dp": there})
    pl.semaphore_wait(barrier, 1 + len(ahead) + (3 if packed else 0))
    halos = [
        send_to(sent, ids_ref, before_ref, halo_s.at[0], halo_r.at[0], {"seq": ahead[0]}),
        send_to(sent, ids_ref, after_ref, halo_s.at[1], halo_r.at[1], {"seq": ahead[-1]}),
    ]

    def halo():
        for copy in halos:
            copy.wait_recv()
        return before_ref[...], after_ref[...]

    rows = ids_ref.shape[1]
    chans = table_ref.shape[1]
    start, limit, total = z * (2 * rows), pos_ref[0], n_seq * 2 * rows
    idm, probs, weights, exchange = forward(
        start, limit, total, halo, sent, ids_ref, table_ref, cw_ref, sw_ref, gain_ref, wq_ref,
        g_ref, pooled_ref, ng_ref, wt_ref, grads_ref, pbuf, sums_buf, wh, wl, r1, r2, sq, rd,
        core_s.at[0], core_r.at[0], core_s.at[1], core_r.at[1], other_core,
    )
    exchange.wait_recv()
    sums = sums_buf[0] + sums_buf[1]
    scale = lax.rsqrt(sums[12:13] / D + EPS)
    pull = scale * scale * scale * (sums[13:14] / D)
    cols = jnp.concatenate([scale, pull, jnp.zeros((6, rows), F32)], axis=0).T
    scale_c, pull_c = cols[:, 0:1], cols[:, 1:2]
    normed[...] = (pooled_ref[...] * scale_c * gain_ref[...]).astype(BF16)

    def tables(put, small_ref):
        table_terms(
            idm, probs, weights, sums, scale, pull, scale_c, pull_c, table_ref, cw_ref, sw_ref,
            gain_ref, pooled_ref, ng_ref, wt_ref, put, small_ref,
        )

    if not packed:
        query_ref, tab_ref, small_ref = outs3

        def put(c, value):
            tab_ref[:, pl.ds(c * CHUNK, CHUNK)] = value

        for c in range(chans // CHUNK):
            at = pl.ds(c * CHUNK, CHUNK)
            query_ref[at, :] = mm(normed[:, at], grads_ref[...], TN).astype(BF16)
        tables(put, small_ref)
        for copy in sent:
            copy.wait_send()
        return

    tab_out, small_out, query_out = outs3
    (
        uq, ut, small, q1, qa1, q2, qa2, q3, t1, ta1, t2, ta2, t3, outq, outt, sb1, sb2,
        s1s, s1r, s2s, s2r, s3s, s3r, qs, qr, tzs, tzr, tds, tdr, m1s, m1r, m2s, m2r,
        u1s, u1r, u2s, u2r, u3s, u3r,
    ) = refs[30:]
    send = functools.partial(send_to, sent)
    first, second = (x, y), (y, x)
    hop1, hop2 = (over_x, over_y), (over_y, over_x)
    piece = [4 * h + 2 * first[h] + second[h] for h in range(2)]
    give1 = [pl.ds(4 * h + 2 * (1 - first[h]), 2) for h in range(2)]
    give2 = [4 * h + 2 * first[h] + 1 - second[h] for h in range(2)]
    block = ahead + [z]

    def query_block(n):
        at = pl.ds(pl.multiple_of(block[n] * 256, 256), 256)
        value = mm(normed[...], grads_ref[:, at], TN).astype(BF16)
        for m in range(8):
            uq[block[n], m] = value[128 * m : 128 * m + 128]
        return [
            send(
                uq.at[block[n], give1[h]], q1.at[h, n], s1s.at[h, n], s1r.at[h, n],
                {"dp": hop1[h]},
            )
            for h in range(2)
        ]

    def put(c, value):
        for m in range(8):
            ut[m, c] = value[32 * m : 32 * m + 32]

    stage1 = {n: query_block(n) for n in (0, 1)}
    tables(put, small)
    small1 = [
        send(small, sb1.at[dp], m1s.at[d], m1r.at[d], {"dp": others[d]}) for d in range(3)
    ]
    sb1[dp] = small[...]
    tab1 = [
        send(ut.at[give1[h]], t1.at[h], u1s.at[h], u1r.at[h], {"dp": hop1[h]}) for h in range(2)
    ]
    stage2 = {}
    stage3 = []

    def relay(n):
        copies = []
        for h in range(2):
            stage1[n][h].wait_recv()
            qa1[h, n] = (
                uq[block[n], give2[h]].astype(F32) + q1[h, n, 1 - second[h]].astype(F32)
            ).astype(BF16)
            copies.append(
                send(qa1.at[h, n], q2.at[h, n], s2s.at[h, n], s2r.at[h, n], {"dp": hop2[h]})
            )
        stage2[n] = copies

    def gathered(n):
        parts = []
        for h in range(2):
            stage2[n][h].wait_recv()
            parts.append(
                uq[block[n], piece[h]].astype(F32)
                + q1[h, n, second[h]].astype(F32)
                + q2[h, n].astype(F32)
            )
        return parts

    def pass_on(n):
        parts = gathered(n)
        for h in range(2):
            qa2[n, h] = parts[h].astype(BF16)
        stage3.append(send(qa2.at[n], q3.at[n], s3s.at[n], s3r.at[n], {"seq": ahead[n]}))

    relay(0)
    stage1[2] = query_block(2)
    relay(1)
    tab2 = []
    for h in range(2):
        tab1[h].wait_recv()
        ta1[h] = (ut[give2[h]].astype(F32) + t1[h, 1 - second[h]].astype(F32)).astype(BF16)
        tab2.append(send(ta1.at[h], t2.at[h], u2s.at[h], u2r.at[h], {"dp": hop2[h]}))
    stage1[3] = query_block(3)
    pass_on(0)
    for copy in small1:
        copy.wait_recv()
    sb2[z] = sb1[0] + sb1[1] + sb1[2] + sb1[3]
    small2 = [
        send(sb2.at[z], sb2.at[z], m2s.at[e], m2r.at[e], {"seq": ahead[e]}) for e in range(3)
    ]
    pass_on(1)
    relay(2)
    for h in range(2):
        tab2[h].wait_recv()
        value = ut[piece[h]].astype(F32) + t1[h, second[h]].astype(F32) + t2[h].astype(F32)
        for zb in range(4):
            ta2[zb, h] = value[zb].astype(BF16)
    tab3 = [
        send(ta2.at[ahead[e]], t3.at[e], u3s.at[e], u3r.at[e], {"seq": ahead[e]})
        for e in range(3)
    ]
    relay(3)
    pass_on(2)
    for copy in tab3:
        copy.wait_recv()
    for h in range(2):
        value = ta2[z, h].astype(F32)
        for e in range(3):
            value = value + t3[e, h].astype(F32)
        outt[piece[h], z] = value.astype(BF16)
    table_z = [
        send(
            outt.at[piece[h], z], outt.at[piece[h], z], tzs.at[e, h], tzr.at[e, h],
            {"seq": ahead[e]},
        )
        for e in range(3)
        for h in range(2)
    ]
    for copy in table_z:
        copy.wait_recv()
    last_t = [
        send(outt.at[piece[h]], outt.at[piece[h]], tds.at[d, h], tdr.at[d, h], {"dp": others[d]})
        for d in range(3)
        for h in range(2)
    ]
    own = gathered(3)
    for copy in stage3:
        copy.wait_recv()
    for h in range(2):
        value = own[h]
        for e in range(3):
            value = value + q3[e, h].astype(F32)
        outq[piece[h]] = value.astype(BF16)
    last = [
        send(outq.at[piece[h]], outq.at[piece[h]], qs.at[d, h], qr.at[d, h], {"dp": others[d]})
        for d in range(3)
        for h in range(2)
    ]
    for copy in small2:
        copy.wait_recv()
    small_out[...] = sb2[0] + sb2[1] + sb2[2] + sb2[3]
    for copy in last:
        copy.wait_recv()
    for m in range(8):
        query_out[128 * m : 128 * m + 128, :] = outq[m]
    for copy in last_t:
        copy.wait_recv()
    for m in range(8):
        for zb in range(4):
            tab_out[32 * m : 32 * m + 32, 256 * zb : 256 * zb + 256] = outt[m, zb]
    for copy in sent:
        copy.wait_send()


def body(
    byte_ids, pad_lengths, table, conv_weight, score_weight, norm_gain, query_weight, query_grad
):
    count = byte_ids.shape[1]
    rows = count // 2
    vocab, chans = table.shape
    width = query_grad.shape[2]
    n_seq = lax.axis_size("seq")
    limit = count * n_seq - pad_lengths
    halves = byte_ids.reshape(rows, 2).T
    packed = (n_seq, lax.axis_size("dp"), chans, width, vocab) == (4, 4, 1024, 1024, 256)
    vm = pl.BlockSpec(memory_space=pltpu.VMEM)
    sm = pl.BlockSpec(memory_space=pltpu.SMEM)
    dma = pltpu.SemaphoreType.DMA
    small_shape = jax.ShapeDtypeStruct((8, chans), F32)
    tab_shape = jax.ShapeDtypeStruct((vocab, chans), BF16)
    if packed:
        shapes = (tab_shape, small_shape, jax.ShapeDtypeStruct((chans, width // 4), BF16))
    else:
        shapes = (jax.ShapeDtypeStruct((chans, width), BF16), tab_shape, small_shape)
    scratch = [
        pltpu.VMEM((rows, chans), F32),
        pltpu.VMEM((rows, chans), F32),
        pltpu.VMEM((3, vocab, rows), BF16),
        pltpu.VMEM((rows, width), BF16),
        pltpu.VMEM((2, 8, vocab), F32),
        pltpu.VMEM((2, 16, rows), F32),
        pltpu.VMEM((3, rows, vocab), BF16),
        pltpu.VMEM((3, rows, vocab), BF16),
        pltpu.VMEM((3, vocab, rows), F32),
        pltpu.VMEM((3, vocab, rows), F32),
        pltpu.VMEM((rows, 128), F32),
        pltpu.VMEM((rows, 128), F32),
        pltpu.VMEM((2, rows), jnp.int32),
        pltpu.VMEM((2, rows), jnp.int32),
        pltpu.VMEM((rows, chans), BF16),
    ] + [dma((2,))] * 4
    if packed:
        scratch += [
            pltpu.VMEM((4, 8, 128, 256), BF16),
            pltpu.VMEM((8, 4, 32, 256), BF16),
            pltpu.VMEM((8, chans), F32),
            pltpu.VMEM((2, 4, 2, 128, 256), BF16),
            pltpu.VMEM((2, 4, 128, 256), BF16),
            pltpu.VMEM((2, 4, 128, 256), BF16),
            pltpu.VMEM((3, 2, 128, 256), BF16),
            pltpu.VMEM((3, 2, 128, 256), BF16),
            pltpu.VMEM((2, 2, 4, 32, 256), BF16),
            pltpu.VMEM((2, 4, 32, 256), BF16),
            pltpu.VMEM((2, 4, 32, 256), BF16),
            pltpu.VMEM((4, 2, 32, 256), BF16),
            pltpu.VMEM((3, 2, 32, 256), BF16),
            pltpu.VMEM((8, 128, 256), BF16),
            pltpu.VMEM((8, 4, 32, 256), BF16),
            pltpu.VMEM((4, 8, chans), F32),
            pltpu.VMEM((4, 8, chans), F32),
        ]
        scratch += (
            [dma((2, 4))] * 4 + [dma((3,))] * 2 + [dma((3, 2))] * 6 + [dma((3,))] * 4
            + [dma((2,))] * 4 + [dma((3,))] * 2
        )
    results = pl.pallas_call(
        functools.partial(kernel, packed, n_seq),
        out_shape=shapes,
        in_specs=[sm] + [vm] * 7,
        out_specs=(vm,) * 3,
        scratch_shapes=scratch,
        compiler_params=pltpu.CompilerParams(collective_id=0, has_side_effects=True),
        name="tokenizer_backward",
    )(
        limit, halves, table, conv_weight, score_weight[None, :], norm_gain[None, :],
        query_weight, query_grad[0],
    )
    if packed:
        tab_out, small_out, query_out = results
    else:
        share = lax.psum_scatter(results[0], "seq", scatter_dimension=1, tiled=True)
        query_out = lax.psum(share, "dp")
        tab_out = lax.psum(results[1], ("dp", "seq"))
        small_out = lax.psum(results[2], ("dp", "seq"))
    return (tab_out, small_out[0:3], small_out[3], small_out[4], query_out)


def solution(mesh):
    return jax.shard_map(
        body,
        mesh=mesh,
        in_specs=(
            P("dp", "seq"),
            P("dp"),
            P(None, "tensor"),
            P(None, "tensor"),
            P("tensor"),
            P("tensor"),
            P("tensor", None),
            P("dp", "seq", None),
        ),
        out_specs=(
            P(None, "tensor"),
            P(None, "tensor"),
            P("tensor"),
            P("tensor"),
            P("tensor", "seq"),
        ),
        check_vma=False,
    )
```

```python
import functools

import jax
import jax.numpy as jnp
from jax import lax
from jax.experimental import pallas as pl
from jax.experimental.pallas import tpu as pltpu
from jax.sharding import PartitionSpec as P

D = 2048
EPS = 1e-06
F32 = jnp.float32
BF16 = jnp.bfloat16
OFFS = range(-2, 4)
CHUNK = 256

NN = (((1,), (0,)), ((), ()))
NT = (((1,), (1,)), ((), ()))
TN = (((0,), (0,)), ((), ()))


def mm(lhs, rhs, dims):
    return lax.dot_general(lhs, rhs, dims, preferred_element_type=F32)


def block_weights(start, total, rows):
    i = lax.broadcasted_iota(jnp.int32, (1, rows), 1)
    even = (i % 2) == 0
    inside = {o: (start + 2 * i + o >= 0) & (start + 2 * i + o < total) for o in OFFS}
    table = []
    for b in range(4):
        for p in range(2):
            row = {}
            for o in OFFS:
                if b == 0:
                    if o == p:
                        row[o] = jnp.where(inside[o], 1.0, 0.0)
                elif b == 1:
                    if o in (0, 1):
                        row[o] = jnp.where(inside[o], 0.5, 0.0)
                elif b == 3:
                    if o in (0, 1):
                        row[o] = jnp.where(inside[o], 0.25, 0.0)
                    else:
                        row[o] = jnp.where(inside[o] & (even if o > 1 else ~even), 0.25, 0.0)
                else:
                    d = o - p
                    if -2 <= d <= 2:
                        r = (start + 2 * i + p) % 3
                        row[o] = jnp.where(inside[o] & (r >= -d) & (r <= 2 - d), 1.0 / 3.0, 0.0)
            table.append(row)
    return table


def spread(idm, rows_of, tap):
    rows = idm.shape[1]
    v = lax.broadcasted_iota(jnp.int32, (256, rows), 0)
    acc = None
    for o in OFFS:
        at = o + tap + 2
        term = jnp.where(idm[at : at + 1, :] == v, rows_of[o], 0.0)
        acc = term if acc is None else acc + term
    return acc


def send_to(sent, src, dst, send_sem, recv_sem, target):
    copy = pltpu.make_async_remote_copy(
        src_ref=src, dst_ref=dst, send_sem=send_sem, recv_sem=recv_sem,
        device_id=target, device_id_type=pl.DeviceIdType.MESH,
    )
    copy.start()
    sent.append(copy)
    return copy


def greet(target):
    pl.semaphore_signal(
        pltpu.get_barrier_semaphore(), inc=1, device_id=target,
        device_id_type=pl.DeviceIdType.MESH,
    )


def split3(value):
    hi = value.astype(BF16)
    rest = value - hi.astype(F32)
    mid = rest.astype(BF16)
    low = (rest - mid.astype(F32)).astype(BF16)
    parts = [hi.astype(F32), mid.astype(F32), low.astype(F32)]
    return jnp.concatenate(parts, axis=0).astype(BF16)


def shifted(own, before, after, by):
    if by == 0:
        return own
    rows = own.shape[1]
    i = lax.broadcasted_iota(jnp.int32, own.shape, 1)
    turn = (-by) % rows
    side = after if by > 0 else before
    outside = (i + by >= rows) if by > 0 else (i + by < 0)
    return jnp.where(outside, pltpu.roll(side, turn, 1), pltpu.roll(own, turn, 1))


def forward(
    start, limit, total, halo, sent, ids_ref, table_ref, cw_ref, sw_ref, gain_ref, wq_ref, g_ref,
    pooled_ref, ng_ref, wt_ref, grads_ref, pbuf, sums_buf,
    wh, wl, r1, r2, sq, rd, psend, precv, ssend, srecv, other_core,
):
    rows = ids_ref.shape[1]
    chans = table_ref.shape[1]
    part = None
    six = split3(
        jnp.concatenate([cw_ref[...] * sw_ref[...], jnp.zeros((5, chans), F32)], axis=0)
    )
    part = mm(six, table_ref[...], NT)
    pbuf[0] = part[0:8] + part[8:16] + part[16:24]
    exchange = send_to(sent, pbuf.at[0], pbuf.at[1], psend, precv, other_core)
    keep = (start + 2 * lax.broadcasted_iota(jnp.int32, g_ref.shape, 0)) < limit
    grads_ref[...] = jnp.where(keep, g_ref[...].astype(F32), 0.0).astype(BF16)
    r1[...] = jnp.zeros_like(r1)
    r2[...] = jnp.zeros_like(r2)
    sq[...] = jnp.zeros_like(sq)
    rd[...] = jnp.zeros_like(rd)
    i = lax.broadcasted_iota(jnp.int32, (1, rows), 1)
    v = lax.broadcasted_iota(jnp.int32, (256, rows), 0)
    before, after = halo()
    own = ids_ref[...]
    lines = []
    for at in range(8):
        j = at - 3
        n, by = j % 2, j // 2
        line = shifted(own[n : n + 1], before[n : n + 1], after[n : n + 1], by)
        byte = start + 2 * i + j
        lines.append(jnp.where((byte >= 0) & (byte < limit), line, -1))
    idm = jnp.concatenate(lines, axis=0)
    exchange.wait_recv()
    p3 = split3(pbuf[0] + pbuf[1])
    picks = []
    for j in range(8):
        hot = jnp.where(idm[j : j + 1, :] == v, 1.0, 0.0).astype(BF16)
        g = mm(p3, hot, NN)
        picks.append(g[0:8] + g[8:16] + g[16:24])
    s = {o: picks[o + 2][0:1] + picks[o + 3][1:2] + picks[o + 4][2:3] for o in OFFS}
    weights = block_weights(start, total, rows)
    expo = []
    for row in weights:
        score = None
        for o in row:
            score = row[o] * s[o] if score is None else score + row[o] * s[o]
        expo.append(jnp.exp(score))
    probs = []
    for n in range(8):
        whole = expo[n % 2] + expo[2 + n % 2] + expo[4 + n % 2] + expo[6 + n % 2]
        probs.append(expo[n] / whole)
    a = {}
    for o in OFFS:
        acc = None
        for n in range(8):
            if o in weights[n]:
                term = probs[n] * weights[n][o]
                acc = term if acc is None else acc + term
        a[o] = 0.5 * acc
    for k in range(3):
        w = spread(idm, a, k)
        wt_ref[k] = w.astype(BF16)
        wf = w.T
        top = wf.astype(BF16)
        wh[k] = top
        wl[k] = (wf - top.astype(F32)).astype(BF16)

    def step(c, carry):
        at = pl.ds(pl.multiple_of(c * CHUNK, CHUNK), CHUNK)
        tab = table_ref[:, at]
        cw = cw_ref[:, at]
        ng = mm(grads_ref[...], wq_ref[at, :], NT)
        pooled = None
        for k in range(3):
            part = cw[k : k + 1] * (mm(wh[k], tab, NN) + mm(wl[k], tab, NN))
            pooled = part if pooled is None else pooled + part
        pooled_ref[:, at] = pooled
        ng_ref[:, at] = ng
        gained = ng * gain_ref[:, at]
        square = pooled * pooled
        inner = pooled * gained
        sq[...] += square[:, 0:128] + square[:, 128:256]
        rd[...] += inner[:, 0:128] + inner[:, 128:256]
        gb = gained.astype(BF16)
        pb = pooled.astype(BF16)
        for k in range(3):
            tk = (tab.astype(F32) * cw[k : k + 1]).astype(BF16)
            r1[k] += mm(tk, gb, NT)
            r2[k] += mm(tk, pb, NT)
        return carry

    lax.fori_loop(0, chans // CHUNK, step, 0)
    out = []
    for r in (r1, r2):
        for o in OFFS:
            acc = None
            for k in range(3):
                at = o + k + 2
                term = jnp.where(idm[at : at + 1, :] == v, r[k], 0.0)
                acc = term if acc is None else acc + term
            out.append(jnp.sum(acc, axis=0, keepdims=True))
    out.append(jnp.sum(sq[...].T, axis=0, keepdims=True))
    out.append(jnp.sum(rd[...].T, axis=0, keepdims=True))
    out.append(jnp.zeros((2, rows), F32))
    sums_buf[0] = jnp.concatenate(out, axis=0)
    exchange = send_to(sent, sums_buf.at[0], sums_buf.at[1], ssend, srecv, other_core)
    return idm, probs, weights, exchange


def table_terms(
    idm, probs, weights, sums, scale, pull, scale_c, pull_c, table_ref, cw_ref, sw_ref, gain_ref,
    pooled_ref, ng_ref, wt_ref, put, small_ref,
):
    chans = table_ref.shape[1]
    q = {o: scale * sums[o + 2 : o + 3] - pull * sums[o + 8 : o + 9] for o in OFFS}
    pgrad = []
    for row in weights:
        acc = None
        for o in row:
            acc = row[o] * q[o] if acc is None else acc + row[o] * q[o]
        pgrad.append(0.5 * acc)
    sgrad = []
    for n in range(8):
        mean = None
        for m in range(n % 2, 8, 2):
            term = probs[m] * pgrad[m]
            mean = term if mean is None else mean + term
        sgrad.append(probs[n] * (pgrad[n] - mean))
    ds = {}
    for o in OFFS:
        acc = None
        for n in range(8):
            if o in weights[n]:
                term = sgrad[n] * weights[n][o]
                acc = term if acc is None else acc + term
        ds[o] = acc
    hist = [jnp.sum(spread(idm, ds, k), axis=1, keepdims=True) for k in range(3)]
    for c in range(chans // CHUNK):
        at = pl.ds(c * CHUNK, CHUNK)
        tab = table_ref[:, at].astype(F32)
        cw = cw_ref[:, at]
        sw = sw_ref[:, at]
        ng = ng_ref[:, at]
        pooled = pooled_ref[:, at]
        gain_term = jnp.sum(ng * pooled * scale_c, axis=0, keepdims=True)
        pg = (ng * gain_ref[:, at] * scale_c - pull_c * pooled).astype(BF16)
        total_t = None
        outs = []
        score = None
        for k in range(3):
            full = mm(wt_ref[k], pg, NN) + hist[k] * sw
            term = cw[k : k + 1] * full
            total_t = term if total_t is None else total_t + term
            outs.append(jnp.sum(full * tab, axis=0, keepdims=True))
            term = cw[k : k + 1] * jnp.sum(hist[k] * tab, axis=0, keepdims=True)
            score = term if score is None else score + term
        put(c, total_t.astype(BF16))
        small_ref[:, at] = jnp.concatenate(
            outs + [score, gain_term, jnp.zeros((3, CHUNK), F32)], axis=0
        )


def kernel(
    packed, n_seq, *refs,
):
    pos_ref, ids_ref, table_ref, cw_ref, sw_ref, gain_ref, wq_ref, g_ref = refs[:8]
    outs3 = refs[8:11]
    (
        pooled_ref, ng_ref, wt_ref, grads_ref, pbuf, sums_buf, wh, wl, r1, r2, sq, rd,
        before_ref, after_ref, normed, core_s, core_r, halo_s, halo_r,
    ) = refs[11:30]
    sent = []
    dp, z, core = lax.axis_index("dp"), lax.axis_index("seq"), lax.axis_index("tensor")
    x, y = dp % 2, dp // 2
    over_x, over_y = y * 2 + (1 - x), (1 - y) * 2 + x
    others = (over_x, over_y, (1 - y) * 2 + (1 - x))
    reach = range(1, 4) if packed else (1, n_seq - 1)
    ahead = [(z + e) % n_seq for e in reach]
    other_core = {"tensor": 1 - core}
    barrier = pltpu.get_barrier_semaphore()
    greet(other_core)
    for there in ahead:
        greet({"seq": there})
    if packed:
        for there in others:
            greet({"dp": there})
    pl.semaphore_wait(barrier, 1 + len(ahead) + (3 if packed else 0))
    halos = [
        send_to(sent, ids_ref, before_ref, halo_s.at[0], halo_r.at[0], {"seq": ahead[0]}),
        send_to(sent, ids_ref, after_ref, halo_s.at[1], halo_r.at[1], {"seq": ahead[-1]}),
    ]

    def halo():
        for copy in halos:
            copy.wait_recv()
        return before_ref[...], after_ref[...]

    rows = ids_ref.shape[1]
    chans = table_ref.shape[1]
    start, limit, total = z * (2 * rows), pos_ref[0], n_seq * 2 * rows
    idm, probs, weights, exchange = forward(
        start, limit, total, halo, sent, ids_ref, table_ref, cw_ref, sw_ref, gain_ref, wq_ref,
        g_ref, pooled_ref, ng_ref, wt_ref, grads_ref, pbuf, sums_buf, wh, wl, r1, r2, sq, rd,
        core_s.at[0], core_r.at[0], core_s.at[1], core_r.at[1], other_core,
    )
    exchange.wait_recv()
    sums = sums_buf[0] + sums_buf[1]
    scale = lax.rsqrt(sums[12:13] / D + EPS)
    pull = scale * scale * scale * (sums[13:14] / D)
    cols = jnp.concatenate([scale, pull, jnp.zeros((6, rows), F32)], axis=0).T
    scale_c, pull_c = cols[:, 0:1], cols[:, 1:2]
    normed[...] = (pooled_ref[...] * scale_c * gain_ref[...]).astype(BF16)

    def tables(put, small_ref):
        table_terms(
            idm, probs, weights, sums, scale, pull, scale_c, pull_c, table_ref, cw_ref, sw_ref,
            gain_ref, pooled_ref, ng_ref, wt_ref, put, small_ref,
        )

    if not packed:
        query_ref, tab_ref, small_ref = outs3

        def put(c, value):
            tab_ref[:, pl.ds(c * CHUNK, CHUNK)] = value

        for c in range(chans // CHUNK):
            at = pl.ds(c * CHUNK, CHUNK)
            query_ref[at, :] = mm(normed[:, at], grads_ref[...], TN).astype(BF16)
        tables(put, small_ref)
        for copy in sent:
            copy.wait_send()
        return

    tab_out, small_out, query_out = outs3
    (
        uq, ut, small, q1, qa1, q2, qa2, q3, t1, ta1, t2, ta2, t3, outq, outt, sb1, sb2,
        s1s, s1r, s2s, s2r, s3s, s3r, qs, qr, tzs, tzr, tds, tdr, m1s, m1r, m2s, m2r,
        u1s, u1r, u2s, u2r, u3s, u3r,
    ) = refs[30:]
    send = functools.partial(send_to, sent)
    first, second = (x, y), (y, x)
    hop1, hop2 = (over_x, over_y), (over_y, over_x)
    piece = [4 * h + 2 * first[h] + second[h] for h in range(2)]
    give1 = [pl.ds(4 * h + 2 * (1 - first[h]), 2) for h in range(2)]
    give2 = [4 * h + 2 * first[h] + 1 - second[h] for h in range(2)]
    block = ahead + [z]

    def query_block(n):
        at = pl.ds(pl.multiple_of(block[n] * 256, 256), 256)
        value = mm(normed[...], grads_ref[:, at], TN).astype(BF16)
        for m in range(8):
            uq[block[n], m] = value[128 * m : 128 * m + 128]
        return [
            send(
                uq.at[block[n], give1[h]], q1.at[h, n], s1s.at[h, n], s1r.at[h, n],
                {"dp": hop1[h]},
            )
            for h in range(2)
        ]

    def put(c, value):
        for m in range(8):
            ut[m, c] = value[32 * m : 32 * m + 32]

    stage1 = {n: query_block(n) for n in (0, 1)}
    tables(put, small)
    small1 = [
        send(small, sb1.at[dp], m1s.at[d], m1r.at[d], {"dp": others[d]}) for d in range(3)
    ]
    sb1[dp] = small[...]
    tab1 = [
        send(ut.at[give1[h]], t1.at[h], u1s.at[h], u1r.at[h], {"dp": hop1[h]}) for h in range(2)
    ]
    for n in (2, 3):
        stage1[n] = query_block(n)
    stage2 = {}
    stage3 = []

    def relay(n):
        copies = []
        for h in range(2):
            stage1[n][h].wait_recv()
            qa1[h, n] = (
                uq[block[n], give2[h]].astype(F32) + q1[h, n, 1 - second[h]].astype(F32)
            ).astype(BF16)
            copies.append(
                send(qa1.at[h, n], q2.at[h, n], s2s.at[h, n], s2r.at[h, n], {"dp": hop2[h]})
            )
        stage2[n] = copies

    def gathered(n):
        parts = []
        for h in range(2):
            stage2[n][h].wait_recv()
            parts.append(
                uq[block[n], piece[h]].astype(F32)
                + q1[h, n, second[h]].astype(F32)
                + q2[h, n].astype(F32)
            )
        return parts

    def pass_on(n):
        parts = gathered(n)
        for h in range(2):
            qa2[n, h] = parts[h].astype(BF16)
        stage3.append(send(qa2.at[n], q3.at[n], s3s.at[n], s3r.at[n], {"seq": ahead[n]}))

    relay(0)
    relay(1)
    pass_on(0)
    tab2 = []
    for h in range(2):
        tab1[h].wait_recv()
        ta1[h] = (ut[give2[h]].astype(F32) + t1[h, 1 - second[h]].astype(F32)).astype(BF16)
        tab2.append(send(ta1.at[h], t2.at[h], u2s.at[h], u2r.at[h], {"dp": hop2[h]}))
    for copy in small1:
        copy.wait_recv()
    sb2[z] = sb1[0] + sb1[1] + sb1[2] + sb1[3]
    small2 = [
        send(sb2.at[z], sb2.at[z], m2s.at[e], m2r.at[e], {"seq": ahead[e]}) for e in range(3)
    ]
    pass_on(1)
    relay(2)
    for h in range(2):
        tab2[h].wait_recv()
        value = ut[piece[h]].astype(F32) + t1[h, second[h]].astype(F32) + t2[h].astype(F32)
        for zb in range(4):
            ta2[zb, h] = value[zb].astype(BF16)
    tab3 = [
        send(ta2.at[ahead[e]], t3.at[e], u3s.at[e], u3r.at[e], {"seq": ahead[e]})
        for e in range(3)
    ]
    relay(3)
    pass_on(2)
    for copy in tab3:
        copy.wait_recv()
    for h in range(2):
        value = ta2[z, h].astype(F32)
        for e in range(3):
            value = value + t3[e, h].astype(F32)
        outt[piece[h], z] = value.astype(BF16)
    table_z = [
        send(
            outt.at[piece[h], z], outt.at[piece[h], z], tzs.at[e, h], tzr.at[e, h],
            {"seq": ahead[e]},
        )
        for e in range(3)
        for h in range(2)
    ]
    for copy in table_z:
        copy.wait_recv()
    last_t = [
        send(outt.at[piece[h]], outt.at[piece[h]], tds.at[d, h], tdr.at[d, h], {"dp": others[d]})
        for d in range(3)
        for h in range(2)
    ]
    own = gathered(3)
    for copy in stage3:
        copy.wait_recv()
    for h in range(2):
        value = own[h]
        for e in range(3):
            value = value + q3[e, h].astype(F32)
        outq[piece[h]] = value.astype(BF16)
    last = [
        send(outq.at[piece[h]], outq.at[piece[h]], qs.at[d, h], qr.at[d, h], {"dp": others[d]})
        for d in range(3)
        for h in range(2)
    ]
    for copy in small2:
        copy.wait_recv()
    small_out[...] = sb2[0] + sb2[1] + sb2[2] + sb2[3]
    for copy in last:
        copy.wait_recv()
    for m in range(8):
        query_out[128 * m : 128 * m + 128, :] = outq[m]
    for copy in last_t:
        copy.wait_recv()
    for m in range(8):
        for zb in range(4):
            tab_out[32 * m : 32 * m + 32, 256 * zb : 256 * zb + 256] = outt[m, zb]
    for copy in sent:
        copy.wait_send()


def body(
    byte_ids, pad_lengths, table, conv_weight, score_weight, norm_gain, query_weight, query_grad
):
    count = byte_ids.shape[1]
    rows = count // 2
    vocab, chans = table.shape
    width = query_grad.shape[2]
    n_seq = lax.axis_size("seq")
    limit = count * n_seq - pad_lengths
    halves = byte_ids.reshape(rows, 2).T
    packed = (n_seq, lax.axis_size("dp"), chans, width, vocab) == (4, 4, 1024, 1024, 256)
    vm = pl.BlockSpec(memory_space=pltpu.VMEM)
    sm = pl.BlockSpec(memory_space=pltpu.SMEM)
    dma = pltpu.SemaphoreType.DMA
    small_shape = jax.ShapeDtypeStruct((8, chans), F32)
    tab_shape = jax.ShapeDtypeStruct((vocab, chans), BF16)
    if packed:
        shapes = (tab_shape, small_shape, jax.ShapeDtypeStruct((chans, width // 4), BF16))
    else:
        shapes = (jax.ShapeDtypeStruct((chans, width), BF16), tab_shape, small_shape)
    scratch = [
        pltpu.VMEM((rows, chans), F32),
        pltpu.VMEM((rows, chans), F32),
        pltpu.VMEM((3, vocab, rows), BF16),
        pltpu.VMEM((rows, width), BF16),
        pltpu.VMEM((2, 8, vocab), F32),
        pltpu.VMEM((2, 16, rows), F32),
        pltpu.VMEM((3, rows, vocab), BF16),
        pltpu.VMEM((3, rows, vocab), BF16),
        pltpu.VMEM((3, vocab, rows), F32),
        pltpu.VMEM((3, vocab, rows), F32),
        pltpu.VMEM((rows, 128), F32),
        pltpu.VMEM((rows, 128), F32),
        pltpu.VMEM((2, rows), jnp.int32),
        pltpu.VMEM((2, rows), jnp.int32),
        pltpu.VMEM((rows, chans), BF16),
    ] + [dma((2,))] * 4
    if packed:
        scratch += [
            pltpu.VMEM((4, 8, 128, 256), BF16),
            pltpu.VMEM((8, 4, 32, 256), BF16),
            pltpu.VMEM((8, chans), F32),
            pltpu.VMEM((2, 4, 2, 128, 256), BF16),
            pltpu.VMEM((2, 4, 128, 256), BF16),
            pltpu.VMEM((2, 4, 128, 256), BF16),
            pltpu.VMEM((3, 2, 128, 256), BF16),
            pltpu.VMEM((3, 2, 128, 256), BF16),
            pltpu.VMEM((2, 2, 4, 32, 256), BF16),
            pltpu.VMEM((2, 4, 32, 256), BF16),
            pltpu.VMEM((2, 4, 32, 256), BF16),
            pltpu.VMEM((4, 2, 32, 256), BF16),
            pltpu.VMEM((3, 2, 32, 256), BF16),
            pltpu.VMEM((8, 128, 256), BF16),
            pltpu.VMEM((8, 4, 32, 256), BF16),
            pltpu.VMEM((4, 8, chans), F32),
            pltpu.VMEM((4, 8, chans), F32),
        ]
        scratch += (
            [dma((2, 4))] * 4 + [dma((3,))] * 2 + [dma((3, 2))] * 6 + [dma((3,))] * 4
            + [dma((2,))] * 4 + [dma((3,))] * 2
        )
    results = pl.pallas_call(
        functools.partial(kernel, packed, n_seq),
        out_shape=shapes,
        in_specs=[sm] + [vm] * 7,
        out_specs=(vm,) * 3,
        scratch_shapes=scratch,
        compiler_params=pltpu.CompilerParams(collective_id=0, has_side_effects=True),
        name="tokenizer_backward",
    )(
        limit, halves, table, conv_weight, score_weight[None, :], norm_gain[None, :],
        query_weight, query_grad[0],
    )
    if packed:
        tab_out, small_out, query_out = results
    else:
        share = lax.psum_scatter(results[0], "seq", scatter_dimension=1, tiled=True)
        query_out = lax.psum(share, "dp")
        tab_out = lax.psum(results[1], ("dp", "seq"))
        small_out = lax.psum(results[2], ("dp", "seq"))
    return (tab_out, small_out[0:3], small_out[3], small_out[4], query_out)


def solution(mesh):
    return jax.shard_map(
        body,
        mesh=mesh,
        in_specs=(
            P("dp", "seq"),
            P("dp"),
            P(None, "tensor"),
            P(None, "tensor"),
            P("tensor"),
            P("tensor"),
            P("tensor", None),
            P("dp", "seq", None),
        ),
        out_specs=(
            P(None, "tensor"),
            P(None, "tensor"),
            P("tensor"),
            P("tensor"),
            P("tensor", "seq"),
        ),
        check_vma=False,
    )
```
